32 devices in a mesh: srow: 8 (over y, x, core), scol: 4 (over z).
Axes of the slice: x: 2, y: 2, z: 4, core: 2. Of those that a mesh axis runs over, the one named last changes fastest.
Arguments:
- patterns: float32 [32, 16, 128, 128], P('srow', 'scol'), may hold values from 0.01 to 800, as said below
- offsets: int32 [32, 16, 2], P('srow', 'scol'), may hold values from 0 to 71, as said below
- object_field: float32 [2, 576, 288], P(None, 'srow', 'scol'), may hold values from -5 to 5
- probe: float32 [2, 2, 128, 128], replicated, may hold values from -6 to 6
Outputs:
- new_object: float32 [2, 576, 288], P(None, 'srow', 'scol')
- new_probe: float32 [2, 2, 128, 128], replicated
The draws below stay inside these ranges and needn't reach their ends.
Inputs may be any that keep to these rules, and one draw needn't show every extreme that they name: `patterns`: patterns are positive. `offsets`: position (r, c) has its centre at tile row 16 * (r mod 4) plus 0 to 23, and tile column 16 * (c mod 4) plus 0 to 23.
All inputs are finite; a program needn't handle non-finite values.
Results may differ from the reference program's by a relative error of at most 0.0003.
Values sent between devices are 32-bit elements; how exact they have to be, the bound alone decides.
A program may use at most 64 MiB of HBM per device.

```python
import math
import jax
import jax.numpy as jnp
from jax import lax

W = 128
MODES = 2
STEP = 16
PAD = 8
PR = 4
PC = 4
OBJ_R = 72
OBJ_C = 72
NPR = 32
NPC = 16
OBJ_ROWS = 576
OBJ_COLS = 288


def draw_patterns(key, part):
    subkeys = jax.random.split(key, 3)
    row_frac = (jnp.arange(NPR, dtype=jnp.float32) + 0.5) / NPR
    col_frac = (jnp.arange(NPC, dtype=jnp.float32) + 0.5) / NPC
    levels = 2.0 * 3.0 ** (0.75 * row_frac[:, None] + 0.25 * col_frac[None, :])
    levels = levels * jax.random.uniform(subkeys[0], (NPR, NPC), jnp.float32, 0.7, 1.4)
    tilt_noise = jnp.clip(0.1 * jax.random.normal(subkeys[1], (2, NPR, NPC), jnp.float32), -0.3, 0.3)
    row_bend = 3.6 * ((row_frac - 0.5) ** 2 - 1.0 / 12.0)
    col_bend = 3.6 * ((col_frac - 0.5) ** 2 - 1.0 / 12.0)
    tilt_row = 0.6 * (row_frac[:, None] - 0.5) + 0.3 * (col_frac[None, :] - 0.5) + row_bend[:, None] + tilt_noise[0]
    tilt_col = -0.3 * (row_frac[:, None] - 0.5) + 0.6 * (col_frac[None, :] - 0.5) + col_bend[None, :] + tilt_noise[1]
    counter = jnp.arange(W, dtype=jnp.int32)
    frequency = ((counter + W // 2) % W - W // 2).astype(jnp.float32) * (2.0 / W)
    ramps = jnp.exp(tilt_row[:, :, None, None] * frequency[None, None, :, None] + tilt_col[:, :, None, None] * frequency[None, None, None, :])
    texture = jax.random.uniform(subkeys[2], (NPR, NPC, W, W), jnp.float32, 0.3, 1.7)
    return levels[:, :, None, None] * ramps * texture


def draw_offsets(key, part):
    jitter = jax.random.randint(key, (NPR, NPC, 2), 0, STEP + PAD, dtype=jnp.int32)
    base_row = jnp.arange(NPR, dtype=jnp.int32) % PR * STEP
    base_col = jnp.arange(NPC, dtype=jnp.int32) % PC * STEP
    drawn = jnp.stack([base_row[:, None] + jitter[:, :, 0], base_col[None, :] + jitter[:, :, 1]], axis=-1)
    drawn = drawn.at[0, 0].set(jnp.zeros((2,), jnp.int32))
    return drawn.at[PR - 1, PC - 1].set(jnp.array([OBJ_R - 1, OBJ_C - 1], dtype=jnp.int32))


def shard_levels(rng, shape, shards, least, high):
    def one(position, shards_of):
        heights = jax.random.uniform(jax.random.fold_in(jax.random.fold_in(rng, 6), position), (shards_of,), jnp.float32, least / len(shards), high / len(shards))
        return jnp.repeat(jnp.exp(heights), shape[position] // shards_of).reshape((-1,) + (1,) * (len(shape) - position - 1))

    level = one(*shards[0])
    for cut in shards[1:]:
        level = level * one(*cut)
    return level


def normal_values(stream_key, dims, scale, most, cuts=(), kind=jnp.bfloat16):
    values = scale * jax.random.normal(stream_key, dims, jnp.float32)
    if cuts:
        values = values * shard_levels(stream_key, dims, cuts, -0.22, 0.18)
    return jnp.clip(values, -most, most).astype(kind)


def setup_inputs(seed: int = 0) -> dict:
    arg_keys = jax.random.split(jax.random.key(seed), 5)
    return {
        "patterns": draw_patterns(jax.random.fold_in(arg_keys[4], 71), 0),
        "offsets": draw_offsets(jax.random.fold_in(arg_keys[4], 71), 0),
        "object_field": normal_values(arg_keys[2], (2, OBJ_ROWS, OBJ_COLS), 0.7, 5.0, ((1, 8), (2, 4)), jnp.float32),
        "probe": normal_values(arg_keys[3], (MODES, 2, W, W), 1.0, 6.0, (), jnp.float32),
    }


obj_rate = 0.2
probe_rate = 0.5
amp_floor = 0.1

def signed_freq(length):
    counter = jnp.arange(length, dtype=jnp.int32)
    return ((counter + length // 2) % length - length // 2).astype(jnp.float32)

def solve_three(matrix, right_side):
    crossed = jnp.stack([jnp.cross(matrix[1], matrix[2]), jnp.cross(matrix[2], matrix[0]), jnp.cross(matrix[0], matrix[1])])
    determ = jnp.sum(matrix[0] * crossed[0])
    return jnp.dot(crossed.T, right_side, precision=lax.Precision.HIGHEST) / determ

def reference(patterns, offsets, object_field, probe):
    highest = lax.Precision.HIGHEST
    frequency = signed_freq(W)
    weights = lax.optimization_barrier(jnp.sum(patterns, axis=(2, 3)))
    com_row = jnp.einsum('abij,i->ab', patterns, frequency, precision=highest) / weights
    com_col = jnp.einsum('abij,j->ab', patterns, frequency, precision=highest) / weights
    row_pos = (jnp.arange(NPR, dtype=jnp.float32) + 0.5) / NPR - 0.5
    col_pos = (jnp.arange(NPC, dtype=jnp.float32) + 0.5) / NPC - 0.5
    basis_set = jnp.stack([jnp.ones((NPR, NPC), jnp.float32), jnp.broadcast_to(row_pos[:, None], (NPR, NPC)), jnp.broadcast_to(col_pos[None, :], (NPR, NPC))])
    centres = jnp.stack([com_row, com_col])
    normal = jnp.einsum('iab,jab,ab->ij', basis_set, basis_set, weights, precision=highest)
    moments = jnp.einsum('iab,kab,ab->ik', basis_set, centres, weights, precision=highest)
    coeffs = solve_three(normal, moments)
    descan = jnp.einsum('iab,ik->kab', basis_set, coeffs, precision=highest)

    def shift_row(row_items):
        pattern_row, shift_r, shift_c = row_items
        spectrum = jnp.fft.fft2(pattern_row)
        phases = 2.0 * math.pi / W * (shift_r[:, None, None] * frequency[None, :, None] + shift_c[:, None, None] * frequency[None, None, :])
        turned = spectrum * lax.complex(jnp.cos(phases), jnp.sin(phases))
        return jnp.sqrt(jnp.maximum(jnp.real(jnp.fft.ifft2(turned)), 0.0))
    targets = lax.map(shift_row, (patterns, descan[0], descan[1]))
    obj_complex = lax.complex(object_field[0], object_field[1])
    probe_modes = lax.complex(probe[:, 0], probe[:, 1])
    pixel_steps = jnp.arange(W, dtype=jnp.int32)
    tile_rows = jnp.arange(NPR, dtype=jnp.int32) // PR * OBJ_R
    tile_cols = jnp.arange(NPC, dtype=jnp.int32) // PC * OBJ_C

    def one_row(carried, row_items):
        grad_obj, grad_probe = carried
        target_row, offset_row, tile_row = row_items
        centre_row = tile_row + offset_row[:, 0]
        centre_col = tile_cols + offset_row[:, 1]
        rows_at = (centre_row[:, None] - W // 2 + pixel_steps[None, :]) % OBJ_ROWS
        cols_at = (centre_col[:, None] - W // 2 + pixel_steps[None, :]) % OBJ_COLS
        window = obj_complex[rows_at[:, :, None], cols_at[:, None, :]]
        exit_waves = probe_modes[None] * window[:, None]
        far_field = jnp.fft.fft2(exit_waves, norm='ortho')
        amplitude = jnp.sqrt(lax.optimization_barrier(jnp.sum(jnp.real(far_field) ** 2 + jnp.imag(far_field) ** 2, axis=1)))
        factor = 1.0 - target_row / jnp.maximum(amplitude, amp_floor)
        back_wave = jnp.fft.ifft2(far_field * factor[:, None], norm='ortho')
        grad_window = lax.optimization_barrier(jnp.sum(jnp.conj(probe_modes)[None] * back_wave, axis=1))
        grad_obj = grad_obj.at[rows_at[:, :, None], cols_at[:, None, :]].add(grad_window)
        grad_probe = grad_probe + lax.optimization_barrier(jnp.sum(jnp.conj(window)[:, None] * back_wave, axis=0))
        return ((grad_obj, grad_probe), None)
    carried, _ = lax.scan(one_row, (jnp.zeros_like(obj_complex), jnp.zeros_like(probe_modes)), (targets, offsets, tile_rows))
    grad_obj, grad_probe = carried
    probe_power = jnp.max(lax.optimization_barrier(jnp.sum(probe * probe, axis=(0, 1))))
    updated_obj = obj_complex - obj_rate * grad_obj / probe_power
    updated_probe = probe_modes - probe_rate * grad_probe / (NPR * NPC)
    new_object = jnp.stack([jnp.real(updated_obj), jnp.imag(updated_obj)])
    new_probe = jnp.stack([jnp.real(updated_probe), jnp.imag(updated_probe)], axis=1)
    return (new_object, new_probe)
```

```python
import functools
import math

import jax
import jax.numpy as jnp
import numpy as np
from jax import lax
from jax.experimental import pallas as pl
from jax.experimental.pallas import tpu as pltpu
from jax.sharding import PartitionSpec as P

MESH = pl.DeviceIdType.MESH
obj_rate = 0.2
probe_rate = 0.5
amp_floor = 0.1
GROUP = 4
MODES = 2
tiny = 1e-30
SCATTER_ROWS = 40
DIRS = [(dr, dc) for dr in (-1, 0, 1) for dc in (-1, 0, 1) if (dr, dc) != (0, 0)]
SIDES = [d for d in DIRS if d[1] != 0]
VERTS = [d for d in DIRS if d[1] == 0]
VMEM = pl.BlockSpec(memory_space=pltpu.VMEM)
SMEM = pl.BlockSpec(memory_space=pltpu.SMEM)
ANY = pl.BlockSpec(memory_space=pl.ANY)


def split_np(table):
    high = table.astype(np.float32).astype(jnp.bfloat16)
    low = (table - high.astype(np.float64)).astype(np.float32).astype(jnp.bfloat16)
    return high, low


def tables(width):
    counter = np.arange(width)
    angles = 2.0 * np.pi / width * ((counter[:, None] * counter[None, :]) % width)
    cos, sin = np.cos(angles), np.sin(angles)
    plus = np.block([[cos, sin], [-sin, cos]])
    minus = np.block([[cos, -sin], [sin, cos]])
    scale = 1.0 / width
    parts = []
    for table in (minus * scale, plus, plus * scale, minus):
        parts.extend(split_np(table))
    shift = np.concatenate([cos, sin], axis=0) * scale
    return np.stack(parts), shift.astype(np.float32)


def split(values):
    high = values.astype(jnp.bfloat16)
    low = (values - high.astype(jnp.float32)).astype(jnp.bfloat16)
    return high, low


def mm(a, b):
    return jnp.dot(a, b, preferred_element_type=jnp.float32)


def signed(index, width):
    half = width // 2
    return jnp.where(index >= half, index - width, index).astype(jnp.float32)


def wrap(index, count):
    return lax.rem(index + count, count)


def greet(n_row, n_col):
    me_r, me_c = lax.axis_index("srow"), lax.axis_index("scol")
    barrier = pltpu.get_barrier_semaphore()

    def signal(row, col):
        pl.semaphore_signal(barrier, inc=1, device_id=(row, col), device_id_type=MESH)

    for k in range(1, n_row):
        signal(wrap(me_r + k, n_row), me_c)
    for k in range(1, n_col):
        signal(me_r, wrap(me_c + k, n_col))
    for dr, dc in DIRS:
        if dr != 0 and dc != 0:
            signal(wrap(me_r + dr, n_row), wrap(me_c + dc, n_col))


def await_greetings(n_row, n_col):
    pl.semaphore_wait(pltpu.get_barrier_semaphore(), n_row - 1 + n_col - 1 + 4)


def copy_to(src, dst, send, recv, row, col):
    return pltpu.make_async_remote_copy(
        src_ref=src,
        dst_ref=dst,
        send_sem=send,
        recv_sem=recv,
        device_id=(row, col),
        device_id_type=MESH,
    )


def halo_copies(n_row, n_col, sides, verts, got_sides, got_verts, send, recv, tile, half):
    me_r, me_c = lax.axis_index("srow"), lax.axis_index("scol")
    copies = []
    for k, (dr, dc) in enumerate(SIDES + VERTS):
        rows = tile if dr == 0 else half
        if dc == 0:
            i = VERTS.index((dr, dc))
            src, dst = verts.at[i], got_verts.at[i]
        else:
            i = SIDES.index((dr, dc))
            src, dst = sides.at[i, pl.ds(0, rows)], got_sides.at[i, pl.ds(0, rows)]
        copies.append(
            copy_to(src, dst, send.at[k], recv.at[k], wrap(me_r + dr, n_row), wrap(me_c + dc, n_col))
        )
    return copies


def lanes_to(values, lanes):
    have = values.shape[-1]
    fill = jnp.zeros(values.shape[:-1] + (lanes - have,), values.dtype)
    return jnp.concatenate([values, fill], axis=-1)


def whole_kernel(
    n_row, n_col, half, positions,
    off_hbm, pat_hbm, obj_hbm, probe_hbm, tab_hbm, shift_hbm, new_obj_ref, new_probe_ref,
    off_ref, pat_ref, obj_ref, probe_ref, tab_ref, shift_ref, load_sems,
    sides, verts, got_sides, got_verts, back_sides, back_verts,
    sums, got_plane, total, got_line,
    ext, far, win, aims, gwin, grad, pgrad, desc_ref, kern, nyq,
    got_p, total_p, got_l, fresh, got_all,
    h_send, h_recv, b_send, b_recv, p_send, p_recv, z_send, z_recv,
    rp_send, rp_recv, rl_send, rl_recv, g_send, g_recv,
):
    greet(n_row, n_col)
    load_obj, load_pat, load_probe, load_tab, load_off, load_shift = [
        pltpu.make_async_copy(src, dst, load_sems.at[k])
        for k, (src, dst) in enumerate([
            (obj_hbm, obj_ref), (pat_hbm, pat_ref), (probe_hbm, probe_ref),
            (tab_hbm, tab_ref), (off_hbm, off_ref), (shift_hbm, shift_ref),
        ])
    ]
    for load in (load_obj, load_pat, load_probe, load_tab, load_off, load_shift):
        load.start()
    me_r, me_c = lax.axis_index("srow"), lax.axis_index("scol")
    pr, pc = off_ref.shape[0], off_ref.shape[2]
    count, width = pat_ref.shape[0], pat_ref.shape[1]
    tile, tile_c = obj_ref.shape[1], obj_ref.shape[2]
    gap, gap_c = tile - half, tile_c - half
    lanes = 2 * width
    ext_rows = ext.shape[2]
    load_obj.wait()
    for i, (dr, dc) in enumerate(SIDES):
        lo = gap if dr == 1 else 0
        rows = tile if dr == 0 else half
        lc = gap_c if dc == 1 else 0
        part = obj_ref[:, lo : lo + rows, :][:, :, lc : lc + half]
        sides[i, 0:rows, :] = jnp.concatenate([part[0], part[1]], axis=-1)
    for i, (dr, dc) in enumerate(VERTS):
        lo = gap if dr == 1 else 0
        verts[i] = lanes_to(obj_ref[:, lo : lo + half, :], width)
    def to_plane(src_of, dst, send, recv):
        copies = []
        for k in range(1, n_row):
            to = wrap(me_r + k, n_row)
            copies.append(copy_to(src_of(to), dst, send.at[k - 1], recv.at[k - 1], to, me_c))
        for copy in copies:
            copy.start()
        return copies

    def to_line(src, dst, send, recv):
        copies = []
        for k in range(1, n_col):
            to = wrap(me_c + k, n_col)
            copies.append(copy_to(src, dst, send.at[k - 1], recv.at[k - 1], me_r, to))
        for copy in copies:
            copy.start()
        return copies

    def finish(copies):
        for copy in copies:
            copy.wait()

    def added(ref, n):
        out = ref[0]
        for k in range(1, n):
            out = out + ref[k]
        return out

    freq_k = signed(lax.broadcasted_iota(jnp.int32, (width, width), 0), width)
    freq_l = signed(lax.broadcasted_iota(jnp.int32, (1, width), 1), width)
    acc = [jnp.zeros((1, width), jnp.float32) for _ in range(9)]
    rows_all, cols_all = float(pr * n_row), float(pc * n_col)
    load_pat.wait()
    for r in range(pr):
        rho = ((me_r * pr + r).astype(jnp.float32) + 0.5) / rows_all - 0.5
        for c in range(pc):
            gam = ((me_c * pc + c).astype(jnp.float32) + 0.5) / cols_all - 0.5
            pattern = pat_ref[r * pc + c]
            col_sum = jnp.sum(pattern, axis=0, keepdims=True)
            row_mom = jnp.sum(pattern * freq_k, axis=0, keepdims=True)
            by_rho, by_gam = col_sum * rho, col_sum * gam
            new = [
                col_sum, by_rho, by_gam, by_rho * rho, by_rho * gam, by_gam * gam,
                row_mom, row_mom * rho, row_mom * gam,
            ]
            acc = [a + b for a, b in zip(acc, new)]
    pieces = acc + [acc[k] * freq_l for k in range(3)]
    stacked = jnp.concatenate(pieces + [jnp.zeros((4, width), jnp.float32)], axis=0)
    mine = jnp.broadcast_to(jnp.sum(stacked, axis=1, keepdims=True), stacked.shape)
    sums[...] = mine
    got_plane[pl.ds(me_r, 1)] = mine[None]
    pad = tile
    blank = jnp.zeros((count, 2, pad, width), jnp.float32)
    gwin[:, :, 0:pad, :] = blank
    gwin[:, :, pad + width :, :] = blank
    pgrad[...] = jnp.zeros_like(pgrad)
    await_greetings(n_row, n_col)
    halo = halo_copies(
        n_row, n_col, sides, verts, got_sides, got_verts, h_send, h_recv, tile, half
    )
    plane = to_plane(lambda to: sums, got_plane.at[me_r], p_send, p_recv)
    for copy in halo:
        copy.start()
    finish(plane)
    here = added(got_plane, n_row)
    total[...] = here
    got_line[pl.ds(me_c, 1)] = here[None]
    line = to_line(total, got_line.at[me_c], z_send, z_recv)
    for load in (load_probe, load_tab, load_off, load_shift):
        load.wait()
    finish(halo)
    own = obj_ref[...]
    for dr, start, rows in ((1, 0, half), (0, half, tile), (-1, half + tile, half)):
        left_part = got_sides[SIDES.index((dr, 1)), 0:rows, :]
        right_part = got_sides[SIDES.index((dr, -1)), 0:rows, :]
        if dr == 0:
            middle = own
        else:
            middle = got_verts[VERTS.index((dr, 0))][:, :, 0:tile_c]
        for part in range(2):
            cut = slice(part * half, part * half + half)
            row = jnp.concatenate([left_part[:, cut], middle[part], right_part[:, cut]], axis=-1)
            row = lanes_to(row, lanes)
            ext[part, 0, start : start + rows, :] = row[:, :width]
            ext[part, 1, start : start + rows, :] = row[:, width:]

    def right(values, k):
        high, low = split(values)
        return mm(high, tab_ref[2 * k]) + mm(low, tab_ref[2 * k]) + mm(high, tab_ref[2 * k + 1])

    def left(values, k):
        high, low = split(values)
        return mm(tab_ref[2 * k], high) + mm(tab_ref[2 * k], low) + mm(tab_ref[2 * k + 1], high)

    def swap(values):
        top = jnp.concatenate([values[:width, :width], values[width:, :width]], axis=1)
        low = jnp.concatenate([values[:width, width:], values[width:, width:]], axis=1)
        return jnp.concatenate([top, low], axis=0)

    lane = lax.broadcasted_iota(jnp.int32, (1, width), 1)

    def corner(place):
        r, c = place // pc, lax.rem(place, pc)
        return off_ref[r, 0, c], off_ref[r, 1, c]

    def window(part, r0, c0):
        shift = lax.rem(width - c0, width)
        first = pltpu.roll(ext[part, 0, pl.ds(r0, width), :], shift, 1)
        second = pltpu.roll(ext[part, 1, pl.ds(r0, width), :], shift, 1)
        return jnp.where(lane < width - c0, first, second)

    def forward(block, carry):
        places = [block * GROUP + g for g in range(GROUP)]
        p0r, p0i, p1r, p1i = (probe_ref[k * width : (k + 1) * width, :] for k in range(4))
        waves = []
        for place in places:
            r0, c0 = corner(place)
            wr, wi = window(0, r0, c0), window(1, r0, c0)
            win[place, 0] = wr
            win[place, 1] = wi
            top = jnp.concatenate([p0r * wr - p0i * wi, p0r * wi + p0i * wr], axis=1)
            low = jnp.concatenate([p1r * wr - p1i * wi, p1r * wi + p1i * wr], axis=1)
            waves.append(jnp.concatenate([top, low], axis=0))
        waves = [right(w, 0) for w in waves]
        for place, w in zip(places, waves):
            far[place] = left(swap(w), 1)
        return carry

    blocks = count // GROUP
    lax.fori_loop(0, blocks, forward, 0)
    finish(line)
    full = added(got_line, n_col)
    t = [full[k : k + 1, :] for k in range(12)]
    m = [[t[0], t[1], t[2]], [t[1], t[3], t[4]], [t[2], t[4], t[5]]]

    def cross(a, b):
        return [
            a[1] * b[2] - a[2] * b[1],
            a[2] * b[0] - a[0] * b[2],
            a[0] * b[1] - a[1] * b[0],
        ]

    crossed = [cross(m[1], m[2]), cross(m[2], m[0]), cross(m[0], m[1])]
    determ = m[0][0] * crossed[0][0] + m[0][1] * crossed[0][1] + m[0][2] * crossed[0][2]
    at = lax.broadcasted_iota(jnp.int32, (count, width), 0)
    at_r, at_c = at // pc, lax.rem(at, pc)
    rho = ((me_r * pr + at_r).astype(jnp.float32) + 0.5) / rows_all - 0.5
    gam = ((me_c * pc + at_c).astype(jnp.float32) + 0.5) / cols_all - 0.5
    pi = math.pi
    cos_tab, sin_tab = shift_ref[0:width, :], shift_ref[width : 2 * width, :]
    hi = lax.Precision.HIGHEST
    waves_of = []
    for axis in range(2):
        rhs = t[6 + 3 * axis : 9 + 3 * axis]
        coeff = [
            (crossed[0][i] * rhs[0] + crossed[1][i] * rhs[1] + crossed[2][i] * rhs[2]) / determ
            for i in range(3)
        ]
        desc = coeff[0] + rho * coeff[1] + gam * coeff[2]
        phase = desc * freq_l * (2.0 * pi / width)
        from_cos = jnp.dot(jnp.cos(phase), cos_tab, precision=hi, preferred_element_type=jnp.float32)
        from_sin = jnp.dot(jnp.sin(phase), sin_tab, precision=hi, preferred_element_type=jnp.float32)
        kern[axis] = from_cos + from_sin if axis == 0 else from_cos - from_sin
        waves_of.append(jnp.sin(desc * pi))
    nyq[...] = waves_of[0] * waves_of[1] * (1.0 / (width * width))
    odd = (
        lax.broadcasted_iota(jnp.int32, (width, width), 0)
        + lax.broadcasted_iota(jnp.int32, (width, width), 1)
    ) & 1
    signs = jnp.where(odd == 1, -1.0, 1.0).astype(jnp.float32)

    def circulant(axis, place):
        row = kern[axis, pl.ds(place, 1), :]
        return pltpu.roll(
            jnp.broadcast_to(row, (width, width)), 0, 1, stride=1, stride_axis=0
        )

    def target(place):
        pattern = pat_ref[place]
        col_high, col_low = split(circulant(1, place))
        row_high, row_low = split(circulant(0, place))
        high, low = split(pattern)
        first = mm(
            jnp.concatenate([high, low, high], axis=1),
            jnp.concatenate([col_high, col_high, col_low], axis=0),
        )
        high, low = split(first)
        second = mm(
            jnp.concatenate([row_high, row_high, row_low], axis=1),
            jnp.concatenate([high, low, high], axis=0),
        )
        alt = jnp.sum(jnp.sum(pattern * signs, axis=0, keepdims=True), axis=1, keepdims=True)
        extra = nyq[pl.ds(place, 1), :] * alt
        return jnp.maximum(second - extra * signs, 0.0)


    def aim(block, carry):
        places = [block * GROUP + g for g in range(GROUP)]
        goals = [target(place) for place in places]
        for place, goal in zip(places, goals):
            aims[place] = goal
        return carry

    def backward(block, carry):
        places = [block * GROUP + g for g in range(GROUP)]
        waves = []
        for place in places:
            f = far[place]
            power = f * f
            power = power[:width] + power[width:]
            power = jnp.maximum(power[:, :width] + power[:, width:], amp_floor * amp_floor)
            goal = aims[place]
            factor = 1.0 - goal * lax.rsqrt(jnp.maximum(goal, tiny) * power)
            factor = jnp.concatenate([factor, factor], axis=1)
            waves.append(jnp.concatenate([f[:width] * factor, f[width:] * factor], axis=0))
        waves = [left(w, 3) for w in waves]
        waves = [right(swap(w), 2) for w in waves]
        sums_of = [[None, None], [None, None]]
        for wave, place in zip(waves, places):
            wr, wi = win[place, 0], win[place, 1]
            gr, gi = None, None
            for mode in range(MODES):
                br = wave[mode * width : (mode + 1) * width, :width]
                bi = wave[mode * width : (mode + 1) * width, width:]
                qr = probe_ref[(2 * mode) * width : (2 * mode + 1) * width, :]
                qi = probe_ref[(2 * mode + 1) * width : (2 * mode + 2) * width, :]
                parts = (wr * br + wi * bi, wr * bi - wi * br)
                for k in range(2):
                    old = sums_of[mode][k]
                    sums_of[mode][k] = parts[k] if old is None else old + parts[k]
                pr_, pi_ = qr * br + qi * bi, qr * bi - qi * br
                gr = pr_ if gr is None else gr + pr_
                gi = pi_ if gi is None else gi + pi_
            gwin[place, 0, pad : pad + width, :] = gr
            gwin[place, 1, pad : pad + width, :] = gi
        for mode in range(MODES):
            for k in range(2):
                pgrad[mode, k * width : (k + 1) * width, :] += sums_of[mode][k]
        return carry

    def scatter_rows(part, at):
        rows = SCATTER_ROWS
        low = jnp.zeros((rows, width), jnp.float32)
        high = jnp.zeros((rows, width), jnp.float32)
        for place in range(count):
            r0, c0 = corner(place)
            piece = pltpu.roll(gwin[place, part, pl.ds(pad - r0 + at, rows), :], c0, 1)
            low = low + jnp.where(lane >= c0, piece, 0.0)
            high = high + jnp.where(lane < c0, piece, 0.0)
        grad[part, pl.ds(at, rows), 0:width] = low
        grad[part, pl.ds(at, rows), width : 2 * width] = high

    def scatter_block(block, carry):
        for part in range(2):
            scatter_rows(part, pl.multiple_of(block * SCATTER_ROWS, SCATTER_ROWS))
        return carry

    chunk = 2 * width // n_row
    here_at = pl.multiple_of(me_r * chunk, chunk)

    def reduce_plane(mode):
        got_p[mode, pl.ds(me_r, 1)] = pgrad[mode, pl.ds(here_at, chunk), :][None]
        return to_plane(
            lambda to: pgrad.at[mode, pl.ds(pl.multiple_of(to * chunk, chunk), chunk)],
            got_p.at[mode, me_r], rp_send.at[mode], rp_recv.at[mode],
        )

    def reduce_line(mode):
        here = added(got_p.at[mode], n_row)
        total_p[mode] = here
        got_l[mode, pl.ds(me_c, 1)] = here[None]
        return to_line(total_p.at[mode], got_l.at[mode, me_c], rl_send.at[mode], rl_recv.at[mode])

    def spread(mode):
        full = added(got_l.at[mode], n_col)
        old = probe_ref[pl.ds(pl.multiple_of(mode * 2 * width + me_r * chunk, chunk), chunk), :]
        done = old - probe_rate * full / positions
        fresh[mode] = done
        got_all[mode, pl.ds(me_r, 1)] = done[None]
        return to_plane(
            lambda to: fresh.at[mode], got_all.at[mode, me_r], g_send.at[mode], g_recv.at[mode]
        )

    lax.fori_loop(0, blocks, aim, 0)
    lax.fori_loop(0, blocks, backward, 0)
    planes = [reduce_plane(mode) for mode in range(MODES)]
    lax.fori_loop(0, ext_rows // SCATTER_ROWS, scatter_block, 0)
    for i, (dr, dc) in enumerate(SIDES):
        start, rows = {-1: (0, half), 0: (half, tile), 1: (half + tile, half)}[dr]
        lc = 0 if dc == -1 else half + tile_c
        band = grad[:, start : start + rows, :][:, :, lc : lc + half]
        sides[i, 0:rows, :] = jnp.concatenate([band[0], band[1]], axis=-1)
    for i, (dr, dc) in enumerate(VERTS):
        start = 0 if dr == -1 else half + tile
        verts[i] = lanes_to(grad[:, start : start + half, :][:, :, half : half + tile_c], width)
    back = halo_copies(
        n_row, n_col, sides, verts, back_sides, back_verts, b_send, b_recv, tile, half
    )
    for copy in back:
        copy.start()
    lines = []
    for mode in range(MODES):
        finish(planes[mode])
        lines.append(reduce_line(mode))
    squares = probe_ref[...]
    squares = squares * squares
    power = squares[0:width]
    for k in range(1, 4):
        power = power + squares[k * width : (k + 1) * width]
    power = jnp.max(jnp.max(power, axis=0, keepdims=True), axis=1, keepdims=True)
    gathers = []
    for mode in range(MODES):
        finish(lines[mode])
        gathers.append(spread(mode))
    finish(back)

    def grad_part(part):
        cut = slice(part * half, part * half + half)
        sums = grad[part, half : half + tile, :][:, half : half + tile_c]
        for dr, dc in SIDES + VERTS:
            rows = tile if dr == 0 else half
            if dc == 0:
                piece = back_verts[VERTS.index((dr, dc)), part][:, 0:tile_c]
            else:
                piece = back_sides[SIDES.index((dr, dc)), 0:rows, :][:, cut]
                fill = jnp.zeros((rows, gap_c), jnp.float32)
                piece = jnp.concatenate([fill, piece] if dc == -1 else [piece, fill], axis=1)
            if dr != 0:
                fill = jnp.zeros((gap, tile_c), jnp.float32)
                piece = jnp.concatenate([fill, piece] if dr == -1 else [piece, fill], axis=0)
            sums = sums + piece
        return sums

    for part in range(2):
        new_obj_ref[part] = obj_ref[part] - obj_rate * grad_part(part) / power
    for mode, copies in enumerate(gathers):
        finish(copies)
        for k in range(n_row):
            at = mode * 2 * width + k * chunk
            new_probe_ref[at : at + chunk, :] = got_all[mode, k]


def settle_kernel(obj_ref, probe_ref, new_obj_ref, new_probe_ref):
    new_obj_ref[...] = obj_ref[...]
    new_probe_ref[...] = probe_ref[...]


def on_device(n_row, n_col, patterns, offsets, object_field, probe):
    pr, pc, width = patterns.shape[0], patterns.shape[1], patterns.shape[2]
    tile, tile_c = object_field.shape[1], object_field.shape[2]
    half = width // 2
    count = pr * pc
    lanes = 2 * width
    f32 = jnp.float32
    dma = pltpu.SemaphoreType.DMA
    side_shape, vert_shape = (len(SIDES), tile, width), (len(VERTS), 2, half, width)
    ext_rows = tile + 2 * half
    chunk = 2 * width // n_row
    tab, shift = tables(width)
    shapes = [
        side_shape, vert_shape, side_shape, vert_shape, side_shape, vert_shape,
        (16, width), (n_row, 16, width), (16, width), (n_col, 16, width),
        (2, 2, ext_rows, width),
        (count, 2 * width, 2 * width),
        (count, 2, width, width),
        (count, width, width),
        (count, 2, width + 2 * tile, width),
        (2, ext_rows, lanes),
        (2, 2 * width, width),
        (2, count, width),
        (2, count, width),
        (count, width),
        (2, n_row, chunk, width),
        (2, chunk, width),
        (2, n_col, chunk, width),
        (2, chunk, width),
        (2, n_row, chunk, width),
    ]
    sems = [
        (8,), (8,), (8,), (8,), (n_row - 1,), (n_row - 1,), (n_col - 1,), (n_col - 1,),
        (2, n_row - 1), (2, n_row - 1), (2, n_col - 1), (2, n_col - 1),
        (2, n_row - 1), (2, n_row - 1),
    ]
    new_object, new_probe = pl.pallas_call(
        functools.partial(whole_kernel, n_row, n_col, half, float(count * n_row * n_col)),
        out_shape=(
            jax.ShapeDtypeStruct((2, tile, tile_c), f32),
            jax.ShapeDtypeStruct((4 * width, width), f32),
        ),
        in_specs=[ANY] * 6,
        out_specs=(VMEM, VMEM),
        scratch_shapes=[
            pltpu.SMEM((pr, 2, pc), jnp.int32),
            pltpu.VMEM((count, width, width), f32),
            pltpu.VMEM((2, tile, tile_c), f32),
            pltpu.VMEM((4 * width, width), f32),
            pltpu.VMEM(tab.shape, jnp.bfloat16),
            pltpu.VMEM(shift.shape, f32),
            dma((6,)),
        ]
        + [pltpu.VMEM(shape, f32) for shape in shapes]
        + [dma(n) for n in sems],
        compiler_params=pltpu.CompilerParams(
            collective_id=0, has_side_effects=True, vmem_limit_bytes=60 * 1024 * 1024
        ),
        name="whole",
    )(
        jnp.transpose(offsets, (0, 2, 1)),
        patterns.reshape(count, width, width),
        object_field,
        probe.reshape(4 * width, width),
        jnp.asarray(tab),
        jnp.asarray(shift),
    )
    new_object, new_probe = pl.pallas_call(
        settle_kernel,
        out_shape=(
            jax.ShapeDtypeStruct((2, tile, tile_c), f32),
            jax.ShapeDtypeStruct((4 * width, width), f32),
        ),
        in_specs=[VMEM] * 2,
        out_specs=(VMEM, VMEM),
        name="settle",
    )(new_object, new_probe)
    return (new_object, new_probe.reshape(probe.shape))


def solution(mesh):
    placed = (P("srow", "scol", None, None), P("srow", "scol", None), P(None, "srow", "scol"), P())
    return jax.shard_map(
        functools.partial(on_device, mesh.shape["srow"], mesh.shape["scol"]),
        mesh=mesh,
        in_specs=placed,
        out_specs=(P(None, "srow", "scol"), P()),
        check_vma=False,
    )
```

```python
import functools
import math

import jax
import jax.numpy as jnp
import numpy as np
from jax import lax
from jax.experimental import pallas as pl
from jax.experimental.pallas import tpu as pltpu
from jax.sharding import PartitionSpec as P

MESH = pl.DeviceIdType.MESH
obj_rate = 0.2
probe_rate = 0.5
amp_floor = 0.1
GROUP = 4
MODES = 2
tiny = 1e-30
SCATTER_ROWS = 40
DIRS = [(dr, dc) for dr in (-1, 0, 1) for dc in (-1, 0, 1) if (dr, dc) != (0, 0)]
SIDES = [d for d in DIRS if d[1] != 0]
VERTS = [d for d in DIRS if d[1] == 0]
VMEM = pl.BlockSpec(memory_space=pltpu.VMEM)
SMEM = pl.BlockSpec(memory_space=pltpu.SMEM)
ANY = pl.BlockSpec(memory_space=pl.ANY)


def split_np(table):
    high = table.astype(np.float32).astype(jnp.bfloat16)
    low = (table - high.astype(np.float64)).astype(np.float32).astype(jnp.bfloat16)
    return high, low


def tables(width):
    counter = np.arange(width)
    angles = 2.0 * np.pi / width * ((counter[:, None] * counter[None, :]) % width)
    cos, sin = np.cos(angles), np.sin(angles)
    plus = np.block([[cos, sin], [-sin, cos]])
    minus = np.block([[cos, -sin], [sin, cos]])
    scale = 1.0 / width
    parts = []
    for table in (minus * scale, plus, plus * scale, minus):
        parts.extend(split_np(table))
    shift = np.concatenate([cos, sin], axis=0) * scale
    return np.stack(parts), shift.astype(np.float32)


def split(values):
    high = values.astype(jnp.bfloat16)
    low = (values - high.astype(jnp.float32)).astype(jnp.bfloat16)
    return high, low


def mm(a, b):
    return jnp.dot(a, b, preferred_element_type=jnp.float32)


def signed(index, width):
    half = width // 2
    return jnp.where(index >= half, index - width, index).astype(jnp.float32)


def wrap(index, count):
    return lax.rem(index + count, count)


def greet(n_row, n_col):
    me_r, me_c = lax.axis_index("srow"), lax.axis_index("scol")
    barrier = pltpu.get_barrier_semaphore()

    def signal(row, col):
        pl.semaphore_signal(barrier, inc=1, device_id=(row, col), device_id_type=MESH)

    for k in range(1, n_row):
        signal(wrap(me_r + k, n_row), me_c)
    for k in range(1, n_col):
        signal(me_r, wrap(me_c + k, n_col))
    for dr, dc in DIRS:
        if dr != 0 and dc != 0:
            signal(wrap(me_r + dr, n_row), wrap(me_c + dc, n_col))


def await_greetings(n_row, n_col):
    pl.semaphore_wait(pltpu.get_barrier_semaphore(), n_row - 1 + n_col - 1 + 4)


def copy_to(src, dst, send, recv, row, col):
    return pltpu.make_async_remote_copy(
        src_ref=src,
        dst_ref=dst,
        send_sem=send,
        recv_sem=recv,
        device_id=(row, col),
        device_id_type=MESH,
    )


def halo_out(n_row, n_col, sides, verts, got_sides, got_verts, send, recv, half):
    me_r, me_c = lax.axis_index("srow"), lax.axis_index("scol")
    toward = 1 - 2 * lax.rem(me_r, 2)
    strips, rest, passed = [], [], []
    for k, dc in enumerate((-1, 1)):
        col = wrap(me_c + dc, n_col)
        i = SIDES.index((0, dc))
        strips.append(copy_to(sides.at[i], got_sides.at[i], send.at[k], recv.at[k], me_r, col))
        i = (1 - toward) * 2 + (dc + 1) // 2
        src, dst = sides.at[i, pl.ds(0, half)], got_sides.at[i, pl.ds(0, half)]
        rest.append(copy_to(src, dst, send.at[2 + k], recv.at[2 + k], wrap(me_r - toward, n_row), col))
    for k, (dr, dc) in enumerate(VERTS):
        src, dst = verts.at[k], got_verts.at[k]
        rest.append(copy_to(src, dst, send.at[4 + k], recv.at[4 + k], wrap(me_r + dr, n_row), me_c))
    gap = sides.shape[1] - half
    lo = pl.multiple_of((1 + toward) // 2 * gap, gap)
    for k, dc in enumerate((-1, 1)):
        src = got_sides.at[SIDES.index((0, dc)), pl.ds(lo, half)]
        dst = got_sides.at[(1 + toward) * 2 + (dc + 1) // 2, pl.ds(0, half)]
        passed.append(copy_to(src, dst, send.at[6 + k], recv.at[6 + k], wrap(me_r + toward, n_row), me_c))
    return strips, rest, passed


def halo_back(n_row, n_col, sides, verts, near, back_sides, back_verts, send, recv, half):
    me_r, me_c = lax.axis_index("srow"), lax.axis_index("scol")
    toward = 1 - 2 * lax.rem(me_r, 2)
    close, far_off = [], []
    for k, dc in enumerate((-1, 1)):
        col = wrap(me_c + dc, n_col)
        src = sides.at[(1 + toward) * 2 + k, pl.ds(0, half)]
        close.append(copy_to(src, near.at[k], send.at[k], recv.at[k], wrap(me_r + toward, n_row), me_c))
        i = (1 - toward) * 2 + k
        src, dst = sides.at[i, pl.ds(0, half)], back_sides.at[i, pl.ds(0, half)]
        far_off.append(copy_to(src, dst, send.at[2 + k], recv.at[2 + k], wrap(me_r - toward, n_row), col))
        i = SIDES.index((0, dc))
        far_off.append(copy_to(sides.at[i], back_sides.at[i], send.at[4 + k], recv.at[4 + k], me_r, col))
    for k, (dr, dc) in enumerate(VERTS):
        src, dst = verts.at[k], back_verts.at[k]
        far_off.append(copy_to(src, dst, send.at[6 + k], recv.at[6 + k], wrap(me_r + dr, n_row), me_c))
    return close, far_off


def lanes_to(values, lanes):
    have = values.shape[-1]
    fill = jnp.zeros(values.shape[:-1] + (lanes - have,), values.dtype)
    return jnp.concatenate([values, fill], axis=-1)


def whole_kernel(
    n_row, n_col, half, positions,
    off_hbm, pat_hbm, obj_hbm, probe_hbm, tab_hbm, shift_hbm, new_obj_ref, new_probe_ref,
    pat_split, alts, off_ref, pat_ref, obj_ref, probe_ref, tab_ref, shift_ref, load_sems,
    sides, verts, got_sides, got_verts, back_sides, back_verts, near,
    sums, got_plane, total, got_line,
    ext, far, win, aims, gwin, grad, pgrad, desc_ref, kern, nyq,
    got_p, total_p, got_l, fresh, got_all,
    h_send, h_recv, b_send, b_recv, p_send, p_recv, z_send, z_recv,
    rp_send, rp_recv, rl_send, rl_recv, g_send, g_recv,
):
    greet(n_row, n_col)
    load_obj, load_pat, load_probe, load_tab, load_off, load_shift = [
        pltpu.make_async_copy(src, dst, load_sems.at[k])
        for k, (src, dst) in enumerate([
            (obj_hbm, obj_ref), (pat_hbm, pat_ref), (probe_hbm, probe_ref),
            (tab_hbm, tab_ref), (off_hbm, off_ref), (shift_hbm, shift_ref),
        ])
    ]
    for load in (load_obj, load_pat, load_probe, load_tab, load_off, load_shift):
        load.start()
    me_r, me_c = lax.axis_index("srow"), lax.axis_index("scol")
    pr, pc = off_ref.shape[0], off_ref.shape[2]
    count, width = pat_ref.shape[0], pat_ref.shape[1]
    tile, tile_c = obj_ref.shape[1], obj_ref.shape[2]
    gap, gap_c = tile - half, tile_c - half
    lanes = 2 * width
    ext_rows = ext.shape[2]
    load_obj.wait()
    for i, (dr, dc) in enumerate(SIDES):
        lo = gap if dr == 1 else 0
        rows = tile if dr == 0 else half
        lc = gap_c if dc == 1 else 0
        part = obj_ref[:, lo : lo + rows, :][:, :, lc : lc + half]
        sides[i, 0:rows, :] = jnp.concatenate([part[0], part[1]], axis=-1)
    for i, (dr, dc) in enumerate(VERTS):
        lo = gap if dr == 1 else 0
        verts[i] = lanes_to(obj_ref[:, lo : lo + half, :], width)
    def to_plane(src_of, dst, send, recv):
        copies = []
        for k in range(1, n_row):
            to = wrap(me_r + k, n_row)
            copies.append(copy_to(src_of(to), dst, send.at[k - 1], recv.at[k - 1], to, me_c))
        for copy in copies:
            copy.start()
        return copies

    def to_line(src, dst, send, recv):
        copies = []
        for k in range(1, n_col):
            to = wrap(me_c + k, n_col)
            copies.append(copy_to(src, dst, send.at[k - 1], recv.at[k - 1], me_r, to))
        for copy in copies:
            copy.start()
        return copies

    def finish(copies):
        for copy in copies:
            copy.wait()

    def added(ref, n):
        out = ref[0]
        for k in range(1, n):
            out = out + ref[k]
        return out

    odd = (
        lax.broadcasted_iota(jnp.int32, (width, width), 0)
        + lax.broadcasted_iota(jnp.int32, (width, width), 1)
    ) & 1
    signs = jnp.where(odd == 1, -1.0, 1.0).astype(jnp.float32)
    freq_k = signed(lax.broadcasted_iota(jnp.int32, (width, width), 0), width)
    freq_l = signed(lax.broadcasted_iota(jnp.int32, (1, width), 1), width)
    acc = [jnp.zeros((1, width), jnp.float32) for _ in range(9)]
    rows_all, cols_all = float(pr * n_row), float(pc * n_col)
    load_pat.wait()
    for r in range(pr):
        rho = ((me_r * pr + r).astype(jnp.float32) + 0.5) / rows_all - 0.5
        for c in range(pc):
            gam = ((me_c * pc + c).astype(jnp.float32) + 0.5) / cols_all - 0.5
            pattern = pat_ref[r * pc + c]
            col_sum = jnp.sum(pattern, axis=0, keepdims=True)
            row_mom = jnp.sum(pattern * freq_k, axis=0, keepdims=True)
            alts[r * pc + c : r * pc + c + 1, :] = jnp.sum(pattern * signs, axis=0, keepdims=True)
            high, low = split(pattern)
            pat_split[r * pc + c] = jnp.concatenate([high, low], axis=1)
            by_rho, by_gam = col_sum * rho, col_sum * gam
            new = [
                col_sum, by_rho, by_gam, by_rho * rho, by_rho * gam, by_gam * gam,
                row_mom, row_mom * rho, row_mom * gam,
            ]
            acc = [a + b for a, b in zip(acc, new)]
    pieces = acc + [acc[k] * freq_l for k in range(3)]
    stacked = jnp.concatenate(pieces + [jnp.zeros((4, width), jnp.float32)], axis=0)
    mine = jnp.broadcast_to(jnp.sum(stacked, axis=1, keepdims=True), stacked.shape)
    sums[...] = mine
    got_plane[pl.ds(me_r, 1)] = mine[None]
    pad = tile
    blank = jnp.zeros((count, 2, pad, width), jnp.float32)
    gwin[:, :, 0:pad, :] = blank
    back_sides[pl.ds(4 * lax.rem(me_r, 2), 2)] = jnp.zeros((2,) + back_sides.shape[1:], jnp.float32)
    gwin[:, :, pad + width :, :] = blank
    await_greetings(n_row, n_col)
    strips, rest, passed = halo_out(
        n_row, n_col, sides, verts, got_sides, got_verts, h_send, h_recv, half
    )
    plane = to_plane(lambda to: sums, got_plane.at[me_r], p_send, p_recv)
    for copy in strips + rest:
        copy.start()
    finish(plane)
    here = added(got_plane, n_row)
    total[...] = here
    got_line[pl.ds(me_c, 1)] = here[None]
    line = to_line(total, got_line.at[me_c], z_send, z_recv)
    for load in (load_probe, load_tab, load_off, load_shift):
        load.wait()
    for strip, onward in zip(strips, passed):
        strip.wait_recv()
        onward.start()
    for strip in strips:
        strip.wait_send()
    finish(rest + passed)
    own = obj_ref[...]
    for dr, start, rows in ((1, 0, half), (0, half, tile), (-1, half + tile, half)):
        left_part = got_sides[SIDES.index((dr, 1)), 0:rows, :]
        right_part = got_sides[SIDES.index((dr, -1)), 0:rows, :]
        if dr == 0:
            middle = own
        else:
            middle = got_verts[VERTS.index((dr, 0))][:, :, 0:tile_c]
        for part in range(2):
            cut = slice(part * half, part * half + half)
            row = jnp.concatenate([left_part[:, cut], middle[part], right_part[:, cut]], axis=-1)
            row = lanes_to(row, lanes)
            ext[part, 0, start : start + rows, :] = row[:, :width]
            ext[part, 1, start : start + rows, :] = row[:, width:]

    def right(values, k):
        high, low = split(values)
        return mm(high, tab_ref[2 * k]) + mm(low, tab_ref[2 * k]) + mm(high, tab_ref[2 * k + 1])

    def left(values, k):
        high, low = split(values)
        return mm(tab_ref[2 * k], high) + mm(tab_ref[2 * k], low) + mm(tab_ref[2 * k + 1], high)

    def swap(values):
        top = jnp.concatenate([values[:width, :width], values[width:, :width]], axis=1)
        low = jnp.concatenate([values[:width, width:], values[width:, width:]], axis=1)
        return jnp.concatenate([top, low], axis=0)

    lane = lax.broadcasted_iota(jnp.int32, (1, width), 1)

    def corner(place):
        r, c = place // pc, lax.rem(place, pc)
        return off_ref[r, 0, c], off_ref[r, 1, c]

    def window(part, r0, c0):
        shift = lax.rem(width - c0, width)
        first = pltpu.roll(ext[part, 0, pl.ds(r0, width), :], shift, 1)
        second = pltpu.roll(ext[part, 1, pl.ds(r0, width), :], shift, 1)
        return jnp.where(lane < width - c0, first, second)

    def forward(block, carry):
        places = [block * GROUP + g for g in range(GROUP)]
        p0r, p0i, p1r, p1i = (probe_ref[k * width : (k + 1) * width, :] for k in range(4))
        waves = []
        for place in places:
            r0, c0 = corner(place)
            wr, wi = window(0, r0, c0), window(1, r0, c0)
            win[place, 0] = wr
            win[place, 1] = wi
            top = jnp.concatenate([p0r * wr - p0i * wi, p0r * wi + p0i * wr], axis=1)
            low = jnp.concatenate([p1r * wr - p1i * wi, p1r * wi + p1i * wr], axis=1)
            waves.append(jnp.concatenate([top, low], axis=0))
        waves = [right(w, 0) for w in waves]
        for place, w in zip(places, waves):
            far[place] = left(swap(w), 1)
        return carry

    blocks = count // GROUP
    lax.fori_loop(0, blocks, forward, 0)
    finish(line)
    full = added(got_line, n_col)
    t = [full[k : k + 1, :] for k in range(12)]
    m = [[t[0], t[1], t[2]], [t[1], t[3], t[4]], [t[2], t[4], t[5]]]

    def cross(a, b):
        return [
            a[1] * b[2] - a[2] * b[1],
            a[2] * b[0] - a[0] * b[2],
            a[0] * b[1] - a[1] * b[0],
        ]

    crossed = [cross(m[1], m[2]), cross(m[2], m[0]), cross(m[0], m[1])]
    determ = m[0][0] * crossed[0][0] + m[0][1] * crossed[0][1] + m[0][2] * crossed[0][2]
    at = lax.broadcasted_iota(jnp.int32, (count, width), 0)
    at_r, at_c = at // pc, lax.rem(at, pc)
    rho = ((me_r * pr + at_r).astype(jnp.float32) + 0.5) / rows_all - 0.5
    gam = ((me_c * pc + at_c).astype(jnp.float32) + 0.5) / cols_all - 0.5
    pi = math.pi
    cos_tab, sin_tab = shift_ref[0:width, :], shift_ref[width : 2 * width, :]
    hi = lax.Precision.HIGHEST
    waves_of = []
    for axis in range(2):
        rhs = t[6 + 3 * axis : 9 + 3 * axis]
        coeff = [
            (crossed[0][i] * rhs[0] + crossed[1][i] * rhs[1] + crossed[2][i] * rhs[2]) / determ
            for i in range(3)
        ]
        desc = coeff[0] + rho * coeff[1] + gam * coeff[2]
        phase = desc * freq_l * (2.0 * pi / width)
        from_cos = jnp.dot(jnp.cos(phase), cos_tab, precision=hi, preferred_element_type=jnp.float32)
        from_sin = jnp.dot(jnp.sin(phase), sin_tab, precision=hi, preferred_element_type=jnp.float32)
        kern[axis] = from_cos + from_sin if axis == 0 else from_cos - from_sin
        waves_of.append(jnp.sin(desc * pi))
    alt = jnp.sum(alts[...], axis=1, keepdims=True)
    nyq[...] = waves_of[0] * waves_of[1] * alt * (1.0 / (width * width))
    def circulant(axis, place):
        row = kern[axis, pl.ds(place, 1), :]
        return pltpu.roll(
            jnp.broadcast_to(row, (width, width)), 0, 1, stride=1, stride_axis=0
        )

    def product(parts, values):
        high, low = split(values)
        top = jnp.concatenate([high, low], axis=1)
        bottom = jnp.concatenate([high, jnp.zeros_like(low)], axis=1)
        both = mm(parts, jnp.concatenate([top, bottom], axis=0))
        return both[:, :width] + both[:, width:]

    def target(place):
        first = product(pat_split[place], circulant(1, place))
        high, low = split(circulant(0, place))
        second = product(jnp.concatenate([high, low], axis=1), first)
        extra = nyq[pl.ds(place, 1), :]
        return jnp.maximum(second - extra * signs, 0.0)


    def aim(block, carry):
        places = [block * GROUP + g for g in range(GROUP)]
        goals = [target(place) for place in places]
        for place, goal in zip(places, goals):
            aims[place] = goal
        return carry

    def backward(block, carry):
        places = [block * GROUP + g for g in range(GROUP)]
        waves = []
        for place in places:
            f = far[place]
            power = f * f
            power = power[:width] + power[width:]
            power = jnp.maximum(power[:, :width] + power[:, width:], amp_floor * amp_floor)
            goal = aims[place]
            factor = 1.0 - goal * lax.rsqrt(jnp.maximum(goal, tiny) * power)
            factor = jnp.concatenate([factor, factor], axis=1)
            waves.append(jnp.concatenate([f[:width] * factor, f[width:] * factor], axis=0))
        waves = [left(w, 3) for w in waves]
        for place, w in zip(places, waves):
            far[place] = w
        return carry

    crow = width // n_row

    def chunk_of(step, carry):
        owner = wrap(me_r + 1 + step, n_row)
        at = pl.multiple_of(owner * crow, crow)
        rows = []
        for place in range(count):
            top = far[place, pl.ds(at, crow), :]
            low = far[place, pl.ds(pl.multiple_of(width + at, crow), crow), :]
            for mode in range(MODES):
                cut = slice(mode * width, (mode + 1) * width)
                rows.append(jnp.concatenate([top[:, cut], low[:, cut]], axis=1))
        waves = right(jnp.concatenate(rows, axis=0), 2)
        q = [probe_ref[pl.ds(pl.multiple_of(k * width + at, crow), crow), :] for k in range(4)]
        added_up = [None] * 4
        for place in range(count):
            wr, wi = win[place, 0, pl.ds(at, crow), :], win[place, 1, pl.ds(at, crow), :]
            gr, gi = None, None
            for mode in range(MODES):
                lo = (place * MODES + mode) * crow
                br, bi = waves[lo : lo + crow, :width], waves[lo : lo + crow, width:]
                parts = (wr * br + wi * bi, wr * bi - wi * br)
                for k in range(2):
                    old = added_up[2 * mode + k]
                    added_up[2 * mode + k] = parts[k] if old is None else old + parts[k]
                qr, qi = q[2 * mode], q[2 * mode + 1]
                pr_, pi_ = qr * br + qi * bi, qr * bi - qi * br
                gr = pr_ if gr is None else gr + pr_
                gi = pi_ if gi is None else gi + pi_
            gwin[place, 0, pl.ds(pad + at, crow), :] = gr
            gwin[place, 1, pl.ds(pad + at, crow), :] = gi
        pgrad[pl.ds(owner, 1)] = jnp.concatenate(added_up, axis=0)[None]

        @pl.when(step < n_row - 1)
        def _():
            plane_copy(step).start()

        return carry

    def plane_copy(step):
        owner = wrap(me_r + 1 + step, n_row)
        return copy_to(
            pgrad.at[owner], got_p.at[me_r], rp_send.at[step], rp_recv.at[step], owner, me_c
        )

    def scatter_rows(part, at):
        rows = SCATTER_ROWS
        low = jnp.zeros((rows, width), jnp.float32)
        high = jnp.zeros((rows, width), jnp.float32)
        for place in range(count):
            r0, c0 = corner(place)
            piece = pltpu.roll(gwin[place, part, pl.ds(pad - r0 + at, rows), :], c0, 1)
            low = low + jnp.where(lane >= c0, piece, 0.0)
            high = high + jnp.where(lane < c0, piece, 0.0)
        grad[part, pl.ds(at, rows), 0:width] = low
        grad[part, pl.ds(at, rows), width : 2 * width] = high

    def scatter_block(block, carry):
        for part in range(2):
            scatter_rows(part, pl.multiple_of(block * SCATTER_ROWS, SCATTER_ROWS))
        return carry

    part_rows = 2 * crow

    def reduce_line(mode, here):
        total_p[mode] = here
        got_l[mode, pl.ds(me_c, 1)] = here[None]
        return to_line(total_p.at[mode], got_l.at[mode, me_c], rl_send.at[mode], rl_recv.at[mode])

    def spread(mode):
        full = added(got_l.at[mode], n_col)
        old = []
        for k in range(2):
            at = pl.multiple_of((2 * mode + k) * width + me_r * crow, crow)
            old.append(probe_ref[pl.ds(at, crow), :])
        done = jnp.concatenate(old, axis=0) - probe_rate * full / positions
        fresh[mode] = done
        got_all[mode, pl.ds(me_r, 1)] = done[None]
        return to_plane(
            lambda to: fresh.at[mode], got_all.at[mode, me_r], g_send.at[mode], g_recv.at[mode]
        )

    lax.fori_loop(0, blocks, aim, 0)
    lax.fori_loop(0, blocks, backward, 0)
    lax.fori_loop(0, n_row, chunk_of, 0)
    lax.fori_loop(0, ext_rows // SCATTER_ROWS, scatter_block, 0)
    for i, (dr, dc) in enumerate(SIDES):
        start, rows = {-1: (0, half), 0: (half, tile), 1: (half + tile, half)}[dr]
        lc = 0 if dc == -1 else half + tile_c
        band = grad[:, start : start + rows, :][:, :, lc : lc + half]
        sides[i, 0:rows, :] = jnp.concatenate([band[0], band[1]], axis=-1)
    for i, (dr, dc) in enumerate(VERTS):
        start = 0 if dr == -1 else half + tile
        verts[i] = lanes_to(grad[:, start : start + half, :][:, :, half : half + tile_c], width)
    close, back = halo_back(
        n_row, n_col, sides, verts, near, back_sides, back_verts, b_send, b_recv, half
    )
    for copy in close:
        copy.start()
    got_p[pl.ds(me_r, 1)] = pgrad[pl.ds(me_r, 1)]
    finish([plane_copy(step) for step in range(n_row - 1)])
    here = added(got_p, n_row)
    lines = [
        reduce_line(mode, here[mode * part_rows : (mode + 1) * part_rows])
        for mode in range(MODES)
    ]
    finish(close)
    lo = pl.multiple_of((2 - 2 * lax.rem(me_r, 2)) // 2 * gap, gap)
    for k, dc in enumerate((-1, 1)):
        sides[SIDES.index((0, dc)), pl.ds(lo, half), :] += near[k]
    for copy in back:
        copy.start()
    squares = probe_ref[...]
    squares = squares * squares
    power = squares[0:width]
    for k in range(1, 4):
        power = power + squares[k * width : (k + 1) * width]
    power = jnp.max(jnp.max(power, axis=0, keepdims=True), axis=1, keepdims=True)
    gathers = []
    for mode in range(MODES):
        finish(lines[mode])
        gathers.append(spread(mode))
    finish(back)

    def grad_part(part):
        cut = slice(part * half, part * half + half)
        sums = grad[part, half : half + tile, :][:, half : half + tile_c]
        for dr, dc in SIDES + VERTS:
            rows = tile if dr == 0 else half
            if dc == 0:
                piece = back_verts[VERTS.index((dr, dc)), part][:, 0:tile_c]
            else:
                piece = back_sides[SIDES.index((dr, dc)), 0:rows, :][:, cut]
                fill = jnp.zeros((rows, gap_c), jnp.float32)
                piece = jnp.concatenate([fill, piece] if dc == -1 else [piece, fill], axis=1)
            if dr != 0:
                fill = jnp.zeros((gap, tile_c), jnp.float32)
                piece = jnp.concatenate([fill, piece] if dr == -1 else [piece, fill], axis=0)
            sums = sums + piece
        return sums

    for part in range(2):
        new_obj_ref[part] = obj_ref[part] - obj_rate * grad_part(part) / power
    for mode, copies in enumerate(gathers):
        finish(copies)
        for k in range(n_row):
            for h in range(2):
                at = (mode * 2 + h) * width + k * crow
                new_probe_ref[at : at + crow, :] = got_all[mode, k, h * crow : (h + 1) * crow]


def on_device(n_row, n_col, patterns, offsets, object_field, probe):
    pr, pc, width = patterns.shape[0], patterns.shape[1], patterns.shape[2]
    tile, tile_c = object_field.shape[1], object_field.shape[2]
    half = width // 2
    count = pr * pc
    lanes = 2 * width
    f32 = jnp.float32
    dma = pltpu.SemaphoreType.DMA
    side_shape, vert_shape = (len(SIDES), tile, width), (len(VERTS), 2, half, width)
    ext_rows = tile + 2 * half
    chunk = 2 * width // n_row
    tab, shift = tables(width)
    shapes = [
        side_shape, vert_shape, side_shape, vert_shape, side_shape, vert_shape, (2, half, width),
        (16, width), (n_row, 16, width), (16, width), (n_col, 16, width),
        (2, 2, ext_rows, width),
        (count, 2 * width, 2 * width),
        (count, 2, width, width),
        (count, width, width),
        (count, 2, width + 2 * tile, width),
        (2, ext_rows, lanes),
        (n_row, 4 * width // n_row, width),
        (2, count, width),
        (2, count, width),
        (count, width),
        (n_row, 4 * width // n_row, width),
        (2, chunk, width),
        (2, n_col, chunk, width),
        (2, chunk, width),
        (2, n_row, chunk, width),
    ]
    sems = [
        (8,), (8,), (8,), (8,), (n_row - 1,), (n_row - 1,), (n_col - 1,), (n_col - 1,),
        (n_row - 1,), (n_row - 1,), (2, n_col - 1), (2, n_col - 1),
        (2, n_row - 1), (2, n_row - 1),
    ]
    new_object, new_probe = pl.pallas_call(
        functools.partial(whole_kernel, n_row, n_col, half, float(count * n_row * n_col)),
        out_shape=(
            pltpu.VMEM((2, tile, tile_c), f32),
            pltpu.VMEM((4 * width, width), f32),
        ),
        in_specs=[ANY] * 6,
        out_specs=(VMEM, VMEM),
        scratch_shapes=[
            pltpu.VMEM((count, width, 2 * width), jnp.bfloat16),
            pltpu.VMEM((count, width), f32),
            pltpu.SMEM((pr, 2, pc), jnp.int32),
            pltpu.VMEM((count, width, width), f32),
            pltpu.VMEM((2, tile, tile_c), f32),
            pltpu.VMEM((4 * width, width), f32),
            pltpu.VMEM(tab.shape, jnp.bfloat16),
            pltpu.VMEM(shift.shape, f32),
            dma((6,)),
        ]
        + [pltpu.VMEM(shape, f32) for shape in shapes]
        + [dma(n) for n in sems],
        compiler_params=pltpu.CompilerParams(
            collective_id=0, has_side_effects=True, vmem_limit_bytes=60 * 1024 * 1024
        ),
        name="whole",
    )(
        jnp.transpose(offsets, (0, 2, 1)),
        patterns.reshape(count, width, width),
        object_field,
        probe.reshape(4 * width, width),
        jnp.asarray(tab),
        jnp.asarray(shift),
    )
    return (new_object, new_probe.reshape(probe.shape))


def solution(mesh):
    placed = (P("srow", "scol", None, None), P("srow", "scol", None), P(None, "srow", "scol"), P())
    return jax.shard_map(
        functools.partial(on_device, mesh.shape["srow"], mesh.shape["scol"]),
        mesh=mesh,
        in_specs=placed,
        out_specs=(P(None, "srow", "scol"), P()),
        check_vma=False,
    )
```

```python
import functools
import math

import jax
import jax.numpy as jnp
import numpy as np
from jax import lax
from jax.experimental import pallas as pl
from jax.experimental.pallas import tpu as pltpu
from jax.sharding import PartitionSpec as P

MESH = pl.DeviceIdType.MESH
obj_rate = 0.2
probe_rate = 0.5
amp_floor = 0.1
GROUP = 4
PAIR = 4
MODES = 2
tiny = 1e-30
SCATTER_ROWS = 40
DIRS = [(dr, dc) for dr in (-1, 0, 1) for dc in (-1, 0, 1) if (dr, dc) != (0, 0)]
SIDES = [d for d in DIRS if d[1] != 0]
VERTS = [d for d in DIRS if d[1] == 0]
VMEM = pl.BlockSpec(memory_space=pltpu.VMEM)
SMEM = pl.BlockSpec(memory_space=pltpu.SMEM)
ANY = pl.BlockSpec(memory_space=pl.ANY)


def split_np(table):
    high = table.astype(np.float32).astype(jnp.bfloat16)
    low = (table - high.astype(np.float64)).astype(np.float32).astype(jnp.bfloat16)
    return high, low


def tables(width):
    counter = np.arange(width)
    angles = 2.0 * np.pi / width * ((counter[:, None] * counter[None, :]) % width)
    cos, sin = np.cos(angles), np.sin(angles)
    plus = np.block([[cos, sin], [-sin, cos]])
    minus = np.block([[cos, -sin], [sin, cos]])
    scale = 1.0 / width
    parts = []
    for table in (minus * scale, plus, plus * scale, minus):
        parts.extend(split_np(table))
    shift = np.concatenate([cos, sin], axis=0) * scale
    return np.stack(parts), shift.astype(np.float32)


def split(values):
    high = values.astype(jnp.bfloat16)
    low = (values - high.astype(jnp.float32)).astype(jnp.bfloat16)
    return high, low


def mm(a, b):
    return jnp.dot(a, b, preferred_element_type=jnp.float32)


def signed(index, width):
    half = width // 2
    return jnp.where(index >= half, index - width, index).astype(jnp.float32)


def wrap(index, count):
    return lax.rem(index + count, count)


def greet(n_row, n_col):
    me_r, me_c = lax.axis_index("srow"), lax.axis_index("scol")
    barrier = pltpu.get_barrier_semaphore()

    def signal(row, col):
        pl.semaphore_signal(barrier, inc=1, device_id=(row, col), device_id_type=MESH)

    for k in range(1, n_row):
        signal(wrap(me_r + k, n_row), me_c)
    for k in range(1, n_col):
        signal(me_r, wrap(me_c + k, n_col))
    for dr, dc in DIRS:
        if dr != 0 and dc != 0:
            signal(wrap(me_r + dr, n_row), wrap(me_c + dc, n_col))


def await_greetings(n_row, n_col):
    pl.semaphore_wait(pltpu.get_barrier_semaphore(), n_row - 1 + n_col - 1 + 4)


def copy_to(src, dst, send, recv, row, col):
    return pltpu.make_async_remote_copy(
        src_ref=src,
        dst_ref=dst,
        send_sem=send,
        recv_sem=recv,
        device_id=(row, col),
        device_id_type=MESH,
    )


def halo_out(n_row, n_col, sides, verts, got_sides, got_verts, send, recv, half):
    me_r, me_c = lax.axis_index("srow"), lax.axis_index("scol")
    toward = 1 - 2 * lax.rem(me_r, 2)
    strips, rest, passed = [], [], []
    for k, dc in enumerate((-1, 1)):
        col = wrap(me_c + dc, n_col)
        i = SIDES.index((0, dc))
        strips.append(copy_to(sides.at[i], got_sides.at[i], send.at[k], recv.at[k], me_r, col))
        i = (1 - toward) * 2 + (dc + 1) // 2
        src, dst = sides.at[i, pl.ds(0, half)], got_sides.at[i, pl.ds(0, half)]
        rest.append(copy_to(src, dst, send.at[2 + k], recv.at[2 + k], wrap(me_r - toward, n_row), col))
    for k, (dr, dc) in enumerate(VERTS):
        src, dst = verts.at[k], got_verts.at[k]
        rest.append(copy_to(src, dst, send.at[4 + k], recv.at[4 + k], wrap(me_r + dr, n_row), me_c))
    gap = sides.shape[1] - half
    lo = pl.multiple_of((1 + toward) // 2 * gap, gap)
    for k, dc in enumerate((-1, 1)):
        src = got_sides.at[SIDES.index((0, dc)), pl.ds(lo, half)]
        dst = got_sides.at[(1 + toward) * 2 + (dc + 1) // 2, pl.ds(0, half)]
        passed.append(copy_to(src, dst, send.at[6 + k], recv.at[6 + k], wrap(me_r + toward, n_row), me_c))
    return strips, rest, passed


def halo_back(n_row, n_col, sides, verts, near, back_sides, back_verts, send, recv, half):
    me_r, me_c = lax.axis_index("srow"), lax.axis_index("scol")
    toward = 1 - 2 * lax.rem(me_r, 2)
    close, far_off = [], []
    for k, dc in enumerate((-1, 1)):
        col = wrap(me_c + dc, n_col)
        src = sides.at[(1 + toward) * 2 + k, pl.ds(0, half)]
        close.append(copy_to(src, near.at[k], send.at[k], recv.at[k], wrap(me_r + toward, n_row), me_c))
        i = (1 - toward) * 2 + k
        src, dst = sides.at[i, pl.ds(0, half)], back_sides.at[i, pl.ds(0, half)]
        far_off.append(copy_to(src, dst, send.at[2 + k], recv.at[2 + k], wrap(me_r - toward, n_row), col))
        i = SIDES.index((0, dc))
        far_off.append(copy_to(sides.at[i], back_sides.at[i], send.at[4 + k], recv.at[4 + k], me_r, col))
    for k, (dr, dc) in enumerate(VERTS):
        src, dst = verts.at[k], back_verts.at[k]
        far_off.append(copy_to(src, dst, send.at[6 + k], recv.at[6 + k], wrap(me_r + dr, n_row), me_c))
    return close, far_off


def lanes_to(values, lanes):
    have = values.shape[-1]
    fill = jnp.zeros(values.shape[:-1] + (lanes - have,), values.dtype)
    return jnp.concatenate([values, fill], axis=-1)


def whole_kernel(
    n_row, n_col, half, positions,
    off_hbm, pat_hbm, obj_hbm, probe_hbm, tab_hbm, shift_hbm, new_obj_ref, new_probe_ref,
    pat_split, alts, off_ref, pat_ref, obj_ref, probe_ref, tab_ref, shift_ref, load_sems,
    sides, verts, got_sides, got_verts, back_sides, back_verts, near,
    sums, got_plane, total, got_line,
    ext, far, win, aims, gwin, grad, pgrad, desc_ref, kern, nyq,
    got_p, total_p, got_l, fresh,
    h_send, h_recv, b_send, b_recv, p_send, p_recv, z_send, z_recv,
    rp_send, rp_recv, rl_send, rl_recv, g_send, g_recv,
):
    greet(n_row, n_col)
    load_obj, load_pat, load_probe, load_tab, load_off, load_shift = [
        pltpu.make_async_copy(src, dst, load_sems.at[k])
        for k, (src, dst) in enumerate([
            (obj_hbm, obj_ref), (pat_hbm, pat_ref), (probe_hbm, probe_ref),
            (tab_hbm, tab_ref), (off_hbm, off_ref), (shift_hbm, shift_ref),
        ])
    ]
    for load in (load_pat, load_obj, load_probe, load_tab, load_off, load_shift):
        load.start()
    me_r, me_c = lax.axis_index("srow"), lax.axis_index("scol")
    pr, pc = off_ref.shape[0], off_ref.shape[2]
    count, width = pat_ref.shape[0], pat_ref.shape[1]
    tile, tile_c = obj_ref.shape[1], obj_ref.shape[2]
    gap, gap_c = tile - half, tile_c - half
    lanes = 2 * width
    ext_rows = ext.shape[2]
    load_obj.wait()
    for i, (dr, dc) in enumerate(SIDES):
        lo = gap if dr == 1 else 0
        rows = tile if dr == 0 else half
        lc = gap_c if dc == 1 else 0
        part = obj_ref[:, lo : lo + rows, :][:, :, lc : lc + half]
        sides[i, 0:rows, :] = jnp.concatenate([part[0], part[1]], axis=-1)
    for i, (dr, dc) in enumerate(VERTS):
        lo = gap if dr == 1 else 0
        verts[i] = lanes_to(obj_ref[:, lo : lo + half, :], width)
    def to_plane(src_of, dst, send, recv):
        copies = []
        for k in range(1, n_row):
            to = wrap(me_r + k, n_row)
            copies.append(copy_to(src_of(to), dst, send.at[k - 1], recv.at[k - 1], to, me_c))
        for copy in copies:
            copy.start()
        return copies

    def to_line(src, dst, send, recv):
        copies = []
        for k in range(1, n_col):
            to = wrap(me_c + k, n_col)
            copies.append(copy_to(src, dst, send.at[k - 1], recv.at[k - 1], me_r, to))
        for copy in copies:
            copy.start()
        return copies

    def finish(copies):
        for copy in copies:
            copy.wait()

    def added(ref, n):
        out = ref[0]
        for k in range(1, n):
            out = out + ref[k]
        return out

    odd = (
        lax.broadcasted_iota(jnp.int32, (width, width), 0)
        + lax.broadcasted_iota(jnp.int32, (width, width), 1)
    ) & 1
    signs = jnp.where(odd == 1, -1.0, 1.0).astype(jnp.float32)
    freq_k = signed(lax.broadcasted_iota(jnp.int32, (width, width), 0), width)
    freq_l = signed(lax.broadcasted_iota(jnp.int32, (1, width), 1), width)
    acc = [jnp.zeros((1, width), jnp.float32) for _ in range(9)]
    rows_all, cols_all = float(pr * n_row), float(pc * n_col)
    load_pat.wait()
    for r in range(pr):
        rho = ((me_r * pr + r).astype(jnp.float32) + 0.5) / rows_all - 0.5
        for c in range(pc):
            gam = ((me_c * pc + c).astype(jnp.float32) + 0.5) / cols_all - 0.5
            pattern = pat_ref[r * pc + c]
            col_sum = jnp.sum(pattern, axis=0, keepdims=True)
            row_mom = jnp.sum(pattern * freq_k, axis=0, keepdims=True)
            by_rho, by_gam = col_sum * rho, col_sum * gam
            new = [
                col_sum, by_rho, by_gam, by_rho * rho, by_rho * gam, by_gam * gam,
                row_mom, row_mom * rho, row_mom * gam,
            ]
            acc = [a + b for a, b in zip(acc, new)]
    pieces = acc + [acc[k] * freq_l for k in range(3)]
    stacked = jnp.concatenate(pieces + [jnp.zeros((4, width), jnp.float32)], axis=0)
    mine = jnp.broadcast_to(jnp.sum(stacked, axis=1, keepdims=True), stacked.shape)
    sums[...] = mine
    got_plane[pl.ds(me_r, 1)] = mine[None]
    await_greetings(n_row, n_col)
    strips, rest, passed = halo_out(
        n_row, n_col, sides, verts, got_sides, got_verts, h_send, h_recv, half
    )
    plane = to_plane(lambda to: sums, got_plane.at[me_r], p_send, p_recv)
    for copy in strips + rest:
        copy.start()
    for place in range(count):
        pattern = pat_ref[place]
        alts[place : place + 1, :] = jnp.sum(pattern * signs, axis=0, keepdims=True)
        high, low = split(pattern)
        pat_split[place] = jnp.concatenate([high, low], axis=1)
    pad = tile
    blank = jnp.zeros((count, 2, pad, width), jnp.float32)
    gwin[:, :, 0:pad, :] = blank
    back_sides[pl.ds(4 * lax.rem(me_r, 2), 2)] = jnp.zeros((2,) + back_sides.shape[1:], jnp.float32)
    gwin[:, :, pad + width :, :] = blank
    for load in (load_probe, load_tab, load_off, load_shift):
        load.wait()
    finish(plane)
    here = added(got_plane, n_row)
    total[...] = here
    got_line[pl.ds(me_c, 1)] = here[None]
    line = to_line(total, got_line.at[me_c], z_send, z_recv)
    for strip, onward in zip(strips, passed):
        strip.wait_recv()
        onward.start()
    for strip in strips:
        strip.wait_send()
    finish(rest + passed)
    own = obj_ref[...]
    for dr, start, rows in ((1, 0, half), (0, half, tile), (-1, half + tile, half)):
        left_part = got_sides[SIDES.index((dr, 1)), 0:rows, :]
        right_part = got_sides[SIDES.index((dr, -1)), 0:rows, :]
        if dr == 0:
            middle = own
        else:
            middle = got_verts[VERTS.index((dr, 0))][:, :, 0:tile_c]
        for part in range(2):
            cut = slice(part * half, part * half + half)
            row = jnp.concatenate([left_part[:, cut], middle[part], right_part[:, cut]], axis=-1)
            row = lanes_to(row, lanes)
            ext[part, 0, start : start + rows, :] = row[:, :width]
            ext[part, 1, start : start + rows, :] = row[:, width:]

    def right(values, k):
        high, low = split(values)
        return mm(high, tab_ref[2 * k]) + mm(low, tab_ref[2 * k]) + mm(high, tab_ref[2 * k + 1])

    def left(values, k):
        high, low = split(values)
        return mm(tab_ref[2 * k], high) + mm(tab_ref[2 * k], low) + mm(tab_ref[2 * k + 1], high)

    def swap(values):
        top = jnp.concatenate([values[:width, :width], values[width:, :width]], axis=1)
        low = jnp.concatenate([values[:width, width:], values[width:, width:]], axis=1)
        return jnp.concatenate([top, low], axis=0)

    lane = lax.broadcasted_iota(jnp.int32, (1, width), 1)

    def corner(place):
        r, c = place // pc, lax.rem(place, pc)
        return off_ref[r, 0, c], off_ref[r, 1, c]

    def window(part, r0, c0):
        shift = lax.rem(width - c0, width)
        first = pltpu.roll(ext[part, 0, pl.ds(r0, width), :], shift, 1)
        second = pltpu.roll(ext[part, 1, pl.ds(r0, width), :], shift, 1)
        return jnp.where(lane < width - c0, first, second)

    def forward(block, carry):
        places = [block * GROUP + g for g in range(GROUP)]
        p0r, p0i, p1r, p1i = (probe_ref[k * width : (k + 1) * width, :] for k in range(4))
        waves = []
        for place in places:
            r0, c0 = corner(place)
            wr, wi = window(0, r0, c0), window(1, r0, c0)
            win[place, 0] = wr
            win[place, 1] = wi
            top = jnp.concatenate([p0r * wr - p0i * wi, p0r * wi + p0i * wr], axis=1)
            low = jnp.concatenate([p1r * wr - p1i * wi, p1r * wi + p1i * wr], axis=1)
            waves.append(jnp.concatenate([top, low], axis=0))
        waves = [right(w, 0) for w in waves]
        for place, w in zip(places, waves):
            far[place] = left(swap(w), 1)
        return carry

    blocks = count // GROUP
    lax.fori_loop(0, blocks // 2, forward, 0)
    finish(line)
    full = added(got_line, n_col)
    t = [full[k : k + 1, :] for k in range(12)]
    m = [[t[0], t[1], t[2]], [t[1], t[3], t[4]], [t[2], t[4], t[5]]]

    def cross(a, b):
        return [
            a[1] * b[2] - a[2] * b[1],
            a[2] * b[0] - a[0] * b[2],
            a[0] * b[1] - a[1] * b[0],
        ]

    crossed = [cross(m[1], m[2]), cross(m[2], m[0]), cross(m[0], m[1])]
    determ = m[0][0] * crossed[0][0] + m[0][1] * crossed[0][1] + m[0][2] * crossed[0][2]
    at = lax.broadcasted_iota(jnp.int32, (count, width), 0)
    at_r, at_c = at // pc, lax.rem(at, pc)
    rho = ((me_r * pr + at_r).astype(jnp.float32) + 0.5) / rows_all - 0.5
    gam = ((me_c * pc + at_c).astype(jnp.float32) + 0.5) / cols_all - 0.5
    pi = math.pi
    cos_tab, sin_tab = shift_ref[0:width, :], shift_ref[width : 2 * width, :]
    hi = lax.Precision.HIGHEST
    waves_of = []
    for axis in range(2):
        rhs = t[6 + 3 * axis : 9 + 3 * axis]
        coeff = [
            (crossed[0][i] * rhs[0] + crossed[1][i] * rhs[1] + crossed[2][i] * rhs[2]) / determ
            for i in range(3)
        ]
        desc = coeff[0] + rho * coeff[1] + gam * coeff[2]
        phase = desc * freq_l * (2.0 * pi / width)
        from_cos = jnp.dot(jnp.cos(phase), cos_tab, precision=hi, preferred_element_type=jnp.float32)
        from_sin = jnp.dot(jnp.sin(phase), sin_tab, precision=hi, preferred_element_type=jnp.float32)
        kern[axis] = from_cos + from_sin if axis == 0 else from_cos - from_sin
        waves_of.append(jnp.sin(desc * pi))
    alt = jnp.sum(alts[...], axis=1, keepdims=True)
    nyq[...] = waves_of[0] * waves_of[1] * alt * (1.0 / (width * width))
    def circulant(axis, place):
        row = kern[axis, pl.ds(place, 1), :]
        return pltpu.roll(
            jnp.broadcast_to(row, (width, width)), 0, 1, stride=1, stride_axis=0
        )

    def product(parts, values):
        high, low = split(values)
        top = jnp.concatenate([high, low], axis=1)
        bottom = jnp.concatenate([high, jnp.zeros_like(low)], axis=1)
        both = mm(parts, jnp.concatenate([top, bottom], axis=0))
        return both[:, :width] + both[:, width:]

    def target(place):
        first = product(pat_split[place], circulant(1, place))
        high, low = split(circulant(0, place))
        second = product(jnp.concatenate([high, low], axis=1), first)
        extra = nyq[pl.ds(place, 1), :]
        return jnp.maximum(second - extra * signs, 0.0)


    def aim(block, carry):
        places = [block * GROUP + g for g in range(GROUP)]
        goals = [target(place) for place in places]
        for place, goal in zip(places, goals):
            aims[place] = goal
        return carry

    def backward(block, carry):
        places = [block * GROUP + g for g in range(GROUP)]
        waves = []
        for place in places:
            f = far[place]
            power = f * f
            power = power[:width] + power[width:]
            power = jnp.maximum(power[:, :width] + power[:, width:], amp_floor * amp_floor)
            goal = aims[place]
            factor = 1.0 - goal * lax.rsqrt(jnp.maximum(goal, tiny) * power)
            factor = jnp.concatenate([factor, factor], axis=1)
            waves.append(jnp.concatenate([f[:width] * factor, f[width:] * factor], axis=0))
        waves = [left(w, 3) for w in waves]
        for place, w in zip(places, waves):
            far[place] = w
        return carry

    crow = width // n_row

    def chunk_of(mode, pair):
        cut = slice(mode * width, (mode + 1) * width)
        steps = [PAIR * pair + k for k in range(PAIR)]
        owners = [wrap(me_r + 1 + step, n_row) for step in steps]
        rows = []
        for owner in owners:
            at = pl.multiple_of(owner * crow, crow)
            for place in range(count):
                top = far[place, pl.ds(at, crow), cut]
                low = far[place, pl.ds(pl.multiple_of(width + at, crow), crow), cut]
                rows.append(jnp.concatenate([top, low], axis=1))
        waves = right(jnp.concatenate(rows, axis=0), 2)
        for n, owner in enumerate(owners):
            at = pl.multiple_of(owner * crow, crow)
            added_up = [None] * 2
            for place in range(count):
                wr, wi = win[place, 0, pl.ds(at, crow), :], win[place, 1, pl.ds(at, crow), :]
                lo = (n * count + place) * crow
                br, bi = waves[lo : lo + crow, :width], waves[lo : lo + crow, width:]
                parts = (wr * br + wi * bi, wr * bi - wi * br)
                for k in range(2):
                    added_up[k] = parts[k] if added_up[k] is None else added_up[k] + parts[k]
                far[place, pl.ds(at, crow), cut] = br
                far[place, pl.ds(pl.multiple_of(width + at, crow), crow), cut] = bi
            pgrad[mode, pl.ds(owner, 1)] = jnp.concatenate(added_up, axis=0)[None]
        for step in steps:

            @pl.when(step < n_row - 1)
            def _():
                plane_copy(mode, step).start()

    def gather_modes(block, carry):
        q = [probe_ref[k * width : (k + 1) * width, :] for k in range(4)]
        for place in [2 * block, 2 * block + 1]:
            gr, gi = None, None
            for mode in range(MODES):
                cut = slice(mode * width, (mode + 1) * width)
                br, bi = far[place, 0:width, cut], far[place, width : 2 * width, cut]
                qr, qi = q[2 * mode], q[2 * mode + 1]
                more_r, more_i = qr * br + qi * bi, qr * bi - qi * br
                gr = more_r if gr is None else gr + more_r
                gi = more_i if gi is None else gi + more_i
            gwin[place, 0, pad : pad + width, :] = gr
            gwin[place, 1, pad : pad + width, :] = gi
        return carry

    def chunk_0(step, carry):
        chunk_of(0, step)
        return carry

    def chunk_1(step, carry):
        chunk_of(1, step)
        return carry

    def plane_copy(mode, step):
        owner = wrap(me_r + 1 + step, n_row)
        return copy_to(
            pgrad.at[mode, owner], got_p.at[mode, me_r],
            rp_send.at[mode, step], rp_recv.at[mode, step], owner, me_c,
        )

    def scatter_rows(part, at):
        rows = SCATTER_ROWS
        low = jnp.zeros((rows, width), jnp.float32)
        high = jnp.zeros((rows, width), jnp.float32)
        for place in range(count):
            r0, c0 = corner(place)
            piece = pltpu.roll(gwin[place, part, pl.ds(pad - r0 + at, rows), :], c0, 1)
            low = low + jnp.where(lane >= c0, piece, 0.0)
            high = high + jnp.where(lane < c0, piece, 0.0)
        grad[part, pl.ds(at, rows), 0:width] = low
        grad[part, pl.ds(at, rows), width : 2 * width] = high

    def scatter_block(block, carry):
        for part in range(2):
            scatter_rows(part, pl.multiple_of(block * SCATTER_ROWS, SCATTER_ROWS))
        return carry

    def reduce_line(mode):
        got_p[mode, pl.ds(me_r, 1)] = pgrad[mode, pl.ds(me_r, 1)]
        finish([plane_copy(mode, step) for step in range(n_row - 1)])
        here = added(got_p.at[mode], n_row)
        total_p[mode] = here
        got_l[mode, pl.ds(me_c, 1)] = here[None]
        return to_line(total_p.at[mode], got_l.at[mode, me_c], rl_send.at[mode], rl_recv.at[mode])

    def spread(mode):
        full = added(got_l.at[mode], n_col)
        mine_at = pl.multiple_of(me_r * crow, crow)
        for k in range(2):
            at = pl.multiple_of((2 * mode + k) * width + mine_at, crow)
            old = probe_ref[pl.ds(at, crow), :]
            done = old - probe_rate * full[k * crow : (k + 1) * crow] / positions
            fresh[mode, k] = done
            new_probe_ref[2 * mode + k, pl.ds(mine_at, crow), :] = done
        return to_plane(
            lambda to: fresh.at[mode],
            new_probe_ref.at[pl.ds(2 * mode, 2), pl.ds(mine_at, crow)],
            g_send.at[mode], g_recv.at[mode],
        )


    def forward_aim(block, carry):
        aim(2 * block - blocks, 0)
        aim(2 * block - blocks + 1, 0)
        return forward(block, carry)

    lax.fori_loop(blocks // 2, blocks, forward_aim, 0)
    lax.fori_loop(0, blocks, backward, 0)
    lax.fori_loop(0, n_row // PAIR, chunk_0, 0)
    lax.fori_loop(0, n_row // PAIR, chunk_1, 0)
    lax.fori_loop(0, count // 2, gather_modes, 0)
    lax.fori_loop(0, ext_rows // SCATTER_ROWS, scatter_block, 0)
    for i, (dr, dc) in enumerate(SIDES):
        start, rows = {-1: (0, half), 0: (half, tile), 1: (half + tile, half)}[dr]
        lc = 0 if dc == -1 else half + tile_c
        band = grad[:, start : start + rows, :][:, :, lc : lc + half]
        sides[i, 0:rows, :] = jnp.concatenate([band[0], band[1]], axis=-1)
    for i, (dr, dc) in enumerate(VERTS):
        start = 0 if dr == -1 else half + tile
        verts[i] = lanes_to(grad[:, start : start + half, :][:, :, half : half + tile_c], width)
    close, back = halo_back(
        n_row, n_col, sides, verts, near, back_sides, back_verts, b_send, b_recv, half
    )
    for copy in close:
        copy.start()
    lines = [reduce_line(mode) for mode in range(MODES)]
    finish(close)
    lo = pl.multiple_of((2 - 2 * lax.rem(me_r, 2)) // 2 * gap, gap)
    for k, dc in enumerate((-1, 1)):
        sides[SIDES.index((0, dc)), pl.ds(lo, half), :] += near[k]
    for copy in back:
        copy.start()
    squares = probe_ref[...]
    squares = squares * squares
    power = squares[0:width]
    for k in range(1, 4):
        power = power + squares[k * width : (k + 1) * width]
    power = jnp.max(jnp.max(power, axis=0, keepdims=True), axis=1, keepdims=True)
    gathers = []
    for mode in range(MODES):
        finish(lines[mode])
        gathers.append(spread(mode))
    finish(back)

    def grad_part(part):
        cut = slice(part * half, part * half + half)
        sums = grad[part, half : half + tile, :][:, half : half + tile_c]
        for dr, dc in SIDES + VERTS:
            rows = tile if dr == 0 else half
            if dc == 0:
                piece = back_verts[VERTS.index((dr, dc)), part][:, 0:tile_c]
            else:
                piece = back_sides[SIDES.index((dr, dc)), 0:rows, :][:, cut]
                fill = jnp.zeros((rows, gap_c), jnp.float32)
                piece = jnp.concatenate([fill, piece] if dc == -1 else [piece, fill], axis=1)
            if dr != 0:
                fill = jnp.zeros((gap, tile_c), jnp.float32)
                piece = jnp.concatenate([fill, piece] if dr == -1 else [piece, fill], axis=0)
            sums = sums + piece
        return sums

    for part in range(2):
        new_obj_ref[part] = obj_ref[part] - obj_rate * grad_part(part) / power
    for copies in gathers:
        finish(copies)


def settle_kernel(obj_ref, probe_ref, new_obj_ref, new_probe_ref, sems):
    copies = [
        pltpu.make_async_copy(obj_ref, new_obj_ref, sems.at[0]),
        pltpu.make_async_copy(probe_ref, new_probe_ref, sems.at[1]),
    ]
    for copy in copies:
        copy.start()
    for copy in copies:
        copy.wait()


def on_device(n_row, n_col, patterns, offsets, object_field, probe):
    pr, pc, width = patterns.shape[0], patterns.shape[1], patterns.shape[2]
    tile, tile_c = object_field.shape[1], object_field.shape[2]
    half = width // 2
    count = pr * pc
    lanes = 2 * width
    f32 = jnp.float32
    dma = pltpu.SemaphoreType.DMA
    side_shape, vert_shape = (len(SIDES), tile, width), (len(VERTS), 2, half, width)
    ext_rows = tile + 2 * half
    chunk = 2 * width // n_row
    tab, shift = tables(width)
    shapes = [
        side_shape, vert_shape, side_shape, vert_shape, side_shape, vert_shape, (2, half, width),
        (16, width), (n_row, 16, width), (16, width), (n_col, 16, width),
        (2, 2, ext_rows, width),
        (count, 2 * width, 2 * width),
        (count, 2, width, width),
        (count, width, width),
        (count, 2, width + 2 * tile, width),
        (2, ext_rows, lanes),
        (2, n_row, chunk, width),
        (2, count, width),
        (2, count, width),
        (count, width),
        (2, n_row, chunk, width),
        (2, chunk, width),
        (2, n_col, chunk, width),
        (2, 2, chunk // 2, width),
    ]
    sems = [
        (8,), (8,), (8,), (8,), (n_row - 1,), (n_row - 1,), (n_col - 1,), (n_col - 1,),
        (2, n_row - 1), (2, n_row - 1), (2, n_col - 1), (2, n_col - 1),
        (2, n_row - 1), (2, n_row - 1),
    ]
    new_object, new_probe = pl.pallas_call(
        functools.partial(whole_kernel, n_row, n_col, half, float(count * n_row * n_col)),
        out_shape=(
            pltpu.VMEM((2, tile, tile_c), f32),
            pltpu.VMEM((4, width, width), f32),
        ),
        in_specs=[ANY] * 6,
        out_specs=(VMEM, VMEM),
        scratch_shapes=[
            pltpu.VMEM((count, width, 2 * width), jnp.bfloat16),
            pltpu.VMEM((count, width), f32),
            pltpu.SMEM((pr, 2, pc), jnp.int32),
            pltpu.VMEM((count, width, width), f32),
            pltpu.VMEM((2, tile, tile_c), f32),
            pltpu.VMEM((4 * width, width), f32),
            pltpu.VMEM(tab.shape, jnp.bfloat16),
            pltpu.VMEM(shift.shape, f32),
            dma((6,)),
        ]
        + [pltpu.VMEM(shape, f32) for shape in shapes]
        + [dma(n) for n in sems],
        compiler_params=pltpu.CompilerParams(
            collective_id=0, has_side_effects=True, vmem_limit_bytes=60 * 1024 * 1024
        ),
        name="whole",
    )(
        jnp.transpose(offsets, (0, 2, 1)),
        patterns.reshape(count, width, width),
        object_field,
        probe.reshape(4 * width, width),
        jnp.asarray(tab),
        jnp.asarray(shift),
    )
    new_object, new_probe = pl.pallas_call(
        settle_kernel,
        out_shape=(
            jax.ShapeDtypeStruct((2, tile, tile_c), f32),
            jax.ShapeDtypeStruct((4, width, width), f32),
        ),
        in_specs=[VMEM] * 2,
        out_specs=(ANY, ANY),
        scratch_shapes=[dma((2,))],
        name="settle",
    )(
        pltpu.with_memory_space_constraint(new_object, pltpu.VMEM),
        pltpu.with_memory_space_constraint(new_probe, pltpu.VMEM),
    )
    return (new_object, new_probe.reshape(probe.shape))


def solution(mesh):
    placed = (P("srow", "scol", None, None), P("srow", "scol", None), P(None, "srow", "scol"), P())
    return jax.shard_map(
        functools.partial(on_device, mesh.shape["srow"], mesh.shape["scol"]),
        mesh=mesh,
        in_specs=placed,
        out_specs=(P(None, "srow", "scol"), P()),
        check_vma=False,
    )
```

```python
import functools
import math

import jax
import jax.numpy as jnp
import numpy as np
from jax import lax
from jax.experimental import pallas as pl
from jax.experimental.pallas import tpu as pltpu
from jax.sharding import PartitionSpec as P

MESH = pl.DeviceIdType.MESH
obj_rate = 0.2
probe_rate = 0.5
amp_floor = 0.1
GROUP = 4
FORWARD = 4
BACKWARD = 16
PAIR = 4
MODES = 2
tiny = 1e-30
SCATTER_ROWS = 40
DIRS = [(dr, dc) for dr in (-1, 0, 1) for dc in (-1, 0, 1) if (dr, dc) != (0, 0)]
SIDES = [d for d in DIRS if d[1] != 0]
VERTS = [d for d in DIRS if d[1] == 0]
VMEM = pl.BlockSpec(memory_space=pltpu.VMEM)
SMEM = pl.BlockSpec(memory_space=pltpu.SMEM)
ANY = pl.BlockSpec(memory_space=pl.ANY)


def split_np(table):
    high = table.astype(np.float32).astype(jnp.bfloat16)
    low = (table - high.astype(np.float64)).astype(np.float32).astype(jnp.bfloat16)
    return high, low


def tables(width):
    counter = np.arange(width)
    angles = 2.0 * np.pi / width * ((counter[:, None] * counter[None, :]) % width)
    cos, sin = np.cos(angles), np.sin(angles)
    plus = np.block([[cos, sin], [-sin, cos]])
    minus = np.block([[cos, -sin], [sin, cos]])
    scale = 1.0 / width
    parts = []
    for table in (minus * scale, plus, plus * scale, minus):
        parts.extend(split_np(table))
    shift = np.concatenate([cos, sin], axis=0) * scale
    return np.stack(parts), shift.astype(np.float32)


def split(values):
    high = values.astype(jnp.bfloat16)
    low = (values - high.astype(jnp.float32)).astype(jnp.bfloat16)
    return high, low


def mm(a, b):
    return jnp.dot(a, b, preferred_element_type=jnp.float32)


def signed(index, width):
    half = width // 2
    return jnp.where(index >= half, index - width, index).astype(jnp.float32)


def wrap(index, count):
    return lax.rem(index + count, count)


def greet(n_row, n_col):
    me_r, me_c = lax.axis_index("srow"), lax.axis_index("scol")
    barrier = pltpu.get_barrier_semaphore()

    def signal(row, col):
        pl.semaphore_signal(barrier, inc=1, device_id=(row, col), device_id_type=MESH)

    for k in range(1, n_row):
        signal(wrap(me_r + k, n_row), me_c)
    for k in range(1, n_col):
        signal(me_r, wrap(me_c + k, n_col))
    for dr, dc in DIRS:
        if dr != 0 and dc != 0:
            signal(wrap(me_r + dr, n_row), wrap(me_c + dc, n_col))


def await_greetings(n_row, n_col):
    pl.semaphore_wait(pltpu.get_barrier_semaphore(), n_row - 1 + n_col - 1 + 4)


def copy_to(src, dst, send, recv, row, col):
    return pltpu.make_async_remote_copy(
        src_ref=src,
        dst_ref=dst,
        send_sem=send,
        recv_sem=recv,
        device_id=(row, col),
        device_id_type=MESH,
    )


def halo_out(n_row, n_col, sides, verts, got_sides, got_verts, send, recv, half):
    me_r, me_c = lax.axis_index("srow"), lax.axis_index("scol")
    toward = 1 - 2 * lax.rem(me_r, 2)
    strips, rest, passed = [], [], []
    for k, dc in enumerate((-1, 1)):
        col = wrap(me_c + dc, n_col)
        i = SIDES.index((0, dc))
        strips.append(copy_to(sides.at[i], got_sides.at[i], send.at[k], recv.at[k], me_r, col))
        i = (1 - toward) * 2 + (dc + 1) // 2
        src, dst = sides.at[i, pl.ds(0, half)], got_sides.at[i, pl.ds(0, half)]
        rest.append(copy_to(src, dst, send.at[2 + k], recv.at[2 + k], wrap(me_r - toward, n_row), col))
    for k, (dr, dc) in enumerate(VERTS):
        src, dst = verts.at[k], got_verts.at[k]
        rest.append(copy_to(src, dst, send.at[4 + k], recv.at[4 + k], wrap(me_r + dr, n_row), me_c))
    gap = sides.shape[1] - half
    lo = pl.multiple_of((1 + toward) // 2 * gap, gap)
    for k, dc in enumerate((-1, 1)):
        src = got_sides.at[SIDES.index((0, dc)), pl.ds(lo, half)]
        dst = got_sides.at[(1 + toward) * 2 + (dc + 1) // 2, pl.ds(0, half)]
        passed.append(copy_to(src, dst, send.at[6 + k], recv.at[6 + k], wrap(me_r + toward, n_row), me_c))
    return strips, rest, passed


def halo_back(n_row, n_col, sides, verts, near, back_sides, back_verts, send, recv, half):
    me_r, me_c = lax.axis_index("srow"), lax.axis_index("scol")
    toward = 1 - 2 * lax.rem(me_r, 2)
    close, far_off = [], []
    for k, dc in enumerate((-1, 1)):
        col = wrap(me_c + dc, n_col)
        src = sides.at[(1 + toward) * 2 + k, pl.ds(0, half)]
        close.append(copy_to(src, near.at[k], send.at[k], recv.at[k], wrap(me_r + toward, n_row), me_c))
        i = (1 - toward) * 2 + k
        src, dst = sides.at[i, pl.ds(0, half)], back_sides.at[i, pl.ds(0, half)]
        far_off.append(copy_to(src, dst, send.at[2 + k], recv.at[2 + k], wrap(me_r - toward, n_row), col))
        i = SIDES.index((0, dc))
        far_off.append(copy_to(sides.at[i], back_sides.at[i], send.at[4 + k], recv.at[4 + k], me_r, col))
    for k, (dr, dc) in enumerate(VERTS):
        src, dst = verts.at[k], back_verts.at[k]
        far_off.append(copy_to(src, dst, send.at[6 + k], recv.at[6 + k], wrap(me_r + dr, n_row), me_c))
    return close, far_off


def lanes_to(values, lanes):
    have = values.shape[-1]
    fill = jnp.zeros(values.shape[:-1] + (lanes - have,), values.dtype)
    return jnp.concatenate([values, fill], axis=-1)


def whole_kernel(
    n_row, n_col, half, positions,
    off_hbm, pat_hbm, obj_hbm, probe_hbm, tab_hbm, shift_hbm, new_obj_ref, new_probe_ref,
    pat_split, alts, off_ref, pat_ref, obj_ref, probe_ref, tab_ref, shift_ref, load_sems,
    sides, verts, got_sides, got_verts, back_sides, back_verts, near,
    sums, got_plane, total, got_line,
    ext, far, win, aims, gwin, grad, pgrad, desc_ref, kern, nyq,
    got_p, total_p, got_l, fresh,
    h_send, h_recv, b_send, b_recv, p_send, p_recv, z_send, z_recv,
    rp_send, rp_recv, rl_send, rl_recv, g_send, g_recv,
):
    greet(n_row, n_col)
    load_obj, load_pat, load_probe, load_tab, load_off, load_shift = [
        pltpu.make_async_copy(src, dst, load_sems.at[k])
        for k, (src, dst) in enumerate([
            (obj_hbm, obj_ref), (pat_hbm, pat_ref), (probe_hbm, probe_ref),
            (tab_hbm, tab_ref), (off_hbm, off_ref), (shift_hbm, shift_ref),
        ])
    ]
    for load in (load_pat, load_obj, load_probe, load_tab, load_off, load_shift):
        load.start()
    me_r, me_c = lax.axis_index("srow"), lax.axis_index("scol")
    pr, pc = off_ref.shape[0], off_ref.shape[2]
    count, width = pat_ref.shape[0], pat_ref.shape[1]
    tile, tile_c = obj_ref.shape[1], obj_ref.shape[2]
    gap, gap_c = tile - half, tile_c - half
    lanes = 2 * width
    ext_rows = ext.shape[2]
    load_obj.wait()
    for i, (dr, dc) in enumerate(SIDES):
        lo = gap if dr == 1 else 0
        rows = tile if dr == 0 else half
        lc = gap_c if dc == 1 else 0
        part = obj_ref[:, lo : lo + rows, :][:, :, lc : lc + half]
        sides[i, 0:rows, :] = jnp.concatenate([part[0], part[1]], axis=-1)
    for i, (dr, dc) in enumerate(VERTS):
        lo = gap if dr == 1 else 0
        verts[i] = lanes_to(obj_ref[:, lo : lo + half, :], width)
    def to_plane(src_of, dst, send, recv):
        copies = []
        for k in range(1, n_row):
            to = wrap(me_r + k, n_row)
            copies.append(copy_to(src_of(to), dst, send.at[k - 1], recv.at[k - 1], to, me_c))
        for copy in copies:
            copy.start()
        return copies

    def to_line(src, dst, send, recv):
        copies = []
        for k in range(1, n_col):
            to = wrap(me_c + k, n_col)
            copies.append(copy_to(src, dst, send.at[k - 1], recv.at[k - 1], me_r, to))
        for copy in copies:
            copy.start()
        return copies

    def finish(copies):
        for copy in copies:
            copy.wait()

    def added(ref, n):
        out = ref[0]
        for k in range(1, n):
            out = out + ref[k]
        return out

    odd = (
        lax.broadcasted_iota(jnp.int32, (width, width), 0)
        + lax.broadcasted_iota(jnp.int32, (width, width), 1)
    ) & 1
    signs = jnp.where(odd == 1, -1.0, 1.0).astype(jnp.float32)
    freq_k = signed(lax.broadcasted_iota(jnp.int32, (width, width), 0), width)
    freq_l = signed(lax.broadcasted_iota(jnp.int32, (1, width), 1), width)
    acc = [jnp.zeros((1, width), jnp.float32) for _ in range(9)]
    rows_all, cols_all = float(pr * n_row), float(pc * n_col)
    load_pat.wait()
    for r in range(pr):
        rho = ((me_r * pr + r).astype(jnp.float32) + 0.5) / rows_all - 0.5
        for c in range(pc):
            gam = ((me_c * pc + c).astype(jnp.float32) + 0.5) / cols_all - 0.5
            pattern = pat_ref[r * pc + c]
            col_sum = jnp.sum(pattern, axis=0, keepdims=True)
            row_mom = jnp.sum(pattern * freq_k, axis=0, keepdims=True)
            by_rho, by_gam = col_sum * rho, col_sum * gam
            new = [
                col_sum, by_rho, by_gam, by_rho * rho, by_rho * gam, by_gam * gam,
                row_mom, row_mom * rho, row_mom * gam,
            ]
            acc = [a + b for a, b in zip(acc, new)]
    pieces = acc + [acc[k] * freq_l for k in range(3)]
    stacked = jnp.concatenate(pieces + [jnp.zeros((4, width), jnp.float32)], axis=0)
    mine = jnp.broadcast_to(jnp.sum(stacked, axis=1, keepdims=True), stacked.shape)
    sums[...] = mine
    got_plane[pl.ds(me_r, 1)] = mine[None]
    await_greetings(n_row, n_col)
    strips, rest, passed = halo_out(
        n_row, n_col, sides, verts, got_sides, got_verts, h_send, h_recv, half
    )
    plane = to_plane(lambda to: sums, got_plane.at[me_r], p_send, p_recv)
    for copy in strips + rest:
        copy.start()
    for place in range(count):
        pattern = pat_ref[place]
        alts[place : place + 1, :] = jnp.sum(pattern * signs, axis=0, keepdims=True)
        high, low = split(pattern)
        pat_split[place] = jnp.concatenate([high, low], axis=1)
    pad = tile
    blank = jnp.zeros((count, 2, pad, width), jnp.float32)
    gwin[:, :, 0:pad, :] = blank
    back_sides[pl.ds(4 * lax.rem(me_r, 2), 2)] = jnp.zeros((2,) + back_sides.shape[1:], jnp.float32)
    gwin[:, :, pad + width :, :] = blank
    for load in (load_probe, load_tab, load_off, load_shift):
        load.wait()
    finish(plane)
    here = added(got_plane, n_row)
    total[...] = here
    got_line[pl.ds(me_c, 1)] = here[None]
    line = to_line(total, got_line.at[me_c], z_send, z_recv)
    for strip, onward in zip(strips, passed):
        strip.wait_recv()
        onward.start()
    for strip in strips:
        strip.wait_send()
    own = obj_ref[...]
    for dr, start, rows in ((0, half, tile), (1, 0, half), (-1, half + tile, half)):
        if dr == 1:
            finish(rest + passed)
        left_part = got_sides[SIDES.index((dr, 1)), 0:rows, :]
        right_part = got_sides[SIDES.index((dr, -1)), 0:rows, :]
        if dr == 0:
            middle = own
        else:
            middle = got_verts[VERTS.index((dr, 0))][:, :, 0:tile_c]
        for part in range(2):
            cut = slice(part * half, part * half + half)
            row = jnp.concatenate([left_part[:, cut], middle[part], right_part[:, cut]], axis=-1)
            row = lanes_to(row, lanes)
            ext[part, 0, start : start + rows, :] = row[:, :width]
            ext[part, 1, start : start + rows, :] = row[:, width:]

    def right(values, k):
        high, low = split(values)
        return mm(high, tab_ref[2 * k]) + mm(low, tab_ref[2 * k]) + mm(high, tab_ref[2 * k + 1])

    def left(values, k):
        high, low = split(values)
        return mm(tab_ref[2 * k], high) + mm(tab_ref[2 * k], low) + mm(tab_ref[2 * k + 1], high)

    def swap(values):
        top = jnp.concatenate([values[:width, :width], values[width:, :width]], axis=1)
        low = jnp.concatenate([values[:width, width:], values[width:, width:]], axis=1)
        return jnp.concatenate([top, low], axis=0)

    lane = lax.broadcasted_iota(jnp.int32, (1, width), 1)

    def corner(place):
        r, c = place // pc, place % pc
        return off_ref[r, 0, c], off_ref[r, 1, c]

    def window(part, r0, c0):
        shift = lax.rem(width - c0, width)
        first = pltpu.roll(ext[part, 0, pl.ds(r0, width), :], shift, 1)
        second = pltpu.roll(ext[part, 1, pl.ds(r0, width), :], shift, 1)
        return jnp.where(lane < width - c0, first, second)

    def forward(block, carry):
        places = [block * FORWARD + g for g in range(FORWARD)]
        p0r, p0i, p1r, p1i = (probe_ref[k * width : (k + 1) * width, :] for k in range(4))
        waves = []
        for place in places:
            r0, c0 = corner(place)
            wr, wi = window(0, r0, c0), window(1, r0, c0)
            win[place, 0] = wr
            win[place, 1] = wi
            top = jnp.concatenate([p0r * wr - p0i * wi, p0r * wi + p0i * wr], axis=1)
            low = jnp.concatenate([p1r * wr - p1i * wi, p1r * wi + p1i * wr], axis=1)
            waves.append(jnp.concatenate([top, low], axis=0))
        waves = [right(w, 0) for w in waves]
        for place, w in zip(places, waves):
            far[place] = left(swap(w), 1)
        return carry

    blocks = count // FORWARD
    forward(0, 0)
    finish(line)
    full = added(got_line, n_col)
    t = [full[k : k + 1, :] for k in range(12)]
    m = [[t[0], t[1], t[2]], [t[1], t[3], t[4]], [t[2], t[4], t[5]]]

    def cross(a, b):
        return [
            a[1] * b[2] - a[2] * b[1],
            a[2] * b[0] - a[0] * b[2],
            a[0] * b[1] - a[1] * b[0],
        ]

    crossed = [cross(m[1], m[2]), cross(m[2], m[0]), cross(m[0], m[1])]
    determ = m[0][0] * crossed[0][0] + m[0][1] * crossed[0][1] + m[0][2] * crossed[0][2]
    at = lax.broadcasted_iota(jnp.int32, (count, width), 0)
    at_r, at_c = at // pc, lax.rem(at, pc)
    rho = ((me_r * pr + at_r).astype(jnp.float32) + 0.5) / rows_all - 0.5
    gam = ((me_c * pc + at_c).astype(jnp.float32) + 0.5) / cols_all - 0.5
    pi = math.pi
    cos_tab, sin_tab = shift_ref[0:width, :], shift_ref[width : 2 * width, :]
    hi = lax.Precision.HIGHEST
    waves_of = []
    for axis in range(2):
        rhs = t[6 + 3 * axis : 9 + 3 * axis]
        coeff = [
            (crossed[0][i] * rhs[0] + crossed[1][i] * rhs[1] + crossed[2][i] * rhs[2]) / determ
            for i in range(3)
        ]
        desc = coeff[0] + rho * coeff[1] + gam * coeff[2]
        phase = desc * freq_l * (2.0 * pi / width)
        from_cos = jnp.dot(jnp.cos(phase), cos_tab, precision=hi, preferred_element_type=jnp.float32)
        from_sin = jnp.dot(jnp.sin(phase), sin_tab, precision=hi, preferred_element_type=jnp.float32)
        kern[axis] = from_cos + from_sin if axis == 0 else from_cos - from_sin
        waves_of.append(jnp.sin(desc * pi))
    alt = jnp.sum(alts[...], axis=1, keepdims=True)
    nyq[...] = waves_of[0] * waves_of[1] * alt * (1.0 / (width * width))
    def circulant(axis, place):
        row = kern[axis, pl.ds(place, 1), :]
        return pltpu.roll(
            jnp.broadcast_to(row, (width, width)), 0, 1, stride=1, stride_axis=0
        )

    def product(parts, values):
        high, low = split(values)
        top = jnp.concatenate([high, low], axis=1)
        bottom = jnp.concatenate([high, jnp.zeros_like(low)], axis=1)
        both = mm(parts, jnp.concatenate([top, bottom], axis=0))
        return both[:, :width] + both[:, width:]

    def target(place):
        first = product(pat_split[place], circulant(1, place))
        high, low = split(circulant(0, place))
        second = product(jnp.concatenate([high, low], axis=1), first)
        extra = nyq[pl.ds(place, 1), :]
        return jnp.maximum(second - extra * signs, 0.0)


    def aim(block, carry):
        places = [block * GROUP + g for g in range(GROUP)]
        goals = [target(place) for place in places]
        for place, goal in zip(places, goals):
            aims[place] = goal
        return carry

    def backward(block, carry):
        places = [block * BACKWARD + g for g in range(BACKWARD)]
        waves = []
        for place in places:
            f = far[place]
            power = f * f
            power = power[:width] + power[width:]
            power = jnp.maximum(power[:, :width] + power[:, width:], amp_floor * amp_floor)
            goal = aims[place]
            factor = 1.0 - goal * lax.rsqrt(jnp.maximum(goal, tiny) * power)
            factor = jnp.concatenate([factor, factor], axis=1)
            waves.append(jnp.concatenate([f[:width] * factor, f[width:] * factor], axis=0))
        waves = [left(w, 3) for w in waves]
        for place, w in zip(places, waves):
            far[place] = w
        return carry

    crow = width // n_row

    def chunk_of(mode, pair):
        cut = slice(mode * width, (mode + 1) * width)
        steps = [PAIR * pair + k for k in range(PAIR)]
        owners = [wrap(me_r + 1 + step, n_row) for step in steps]
        rows = []
        for owner in owners:
            at = pl.multiple_of(owner * crow, crow)
            for place in range(count):
                top = far[place, pl.ds(at, crow), cut]
                low = far[place, pl.ds(pl.multiple_of(width + at, crow), crow), cut]
                rows.append(jnp.concatenate([top, low], axis=1))
        waves = right(jnp.concatenate(rows, axis=0), 2)
        for n, owner in enumerate(owners):
            at = pl.multiple_of(owner * crow, crow)
            added_up = [None] * 2
            for place in range(count):
                wr, wi = win[place, 0, pl.ds(at, crow), :], win[place, 1, pl.ds(at, crow), :]
                lo = (n * count + place) * crow
                br, bi = waves[lo : lo + crow, :width], waves[lo : lo + crow, width:]
                parts = (wr * br + wi * bi, wr * bi - wi * br)
                for k in range(2):
                    added_up[k] = parts[k] if added_up[k] is None else added_up[k] + parts[k]
                far[place, pl.ds(at, crow), cut] = br
                far[place, pl.ds(pl.multiple_of(width + at, crow), crow), cut] = bi
            pgrad[mode, pl.ds(owner, 1)] = jnp.concatenate(added_up, axis=0)[None]
        for step in steps:

            @pl.when(step < n_row - 1)
            def _():
                plane_copy(mode, step).start()

    def gather_modes(block, carry):
        q = [probe_ref[k * width : (k + 1) * width, :] for k in range(4)]
        for place in [2 * block, 2 * block + 1]:
            gr, gi = None, None
            for mode in range(MODES):
                cut = slice(mode * width, (mode + 1) * width)
                br, bi = far[place, 0:width, cut], far[place, width : 2 * width, cut]
                qr, qi = q[2 * mode], q[2 * mode + 1]
                more_r, more_i = qr * br + qi * bi, qr * bi - qi * br
                gr = more_r if gr is None else gr + more_r
                gi = more_i if gi is None else gi + more_i
            gwin[place, 0, pad : pad + width, :] = gr
            gwin[place, 1, pad : pad + width, :] = gi
        return carry

    def chunk_0(step, carry):
        chunk_of(0, step)
        return carry

    def chunk_1(step, carry):
        chunk_of(1, step)
        return carry

    def plane_copy(mode, step):
        owner = wrap(me_r + 1 + step, n_row)
        return copy_to(
            pgrad.at[mode, owner], got_p.at[mode, me_r],
            rp_send.at[mode, step], rp_recv.at[mode, step], owner, me_c,
        )

    def scatter_rows(part, at):
        rows = SCATTER_ROWS
        low = jnp.zeros((rows, width), jnp.float32)
        high = jnp.zeros((rows, width), jnp.float32)
        for place in range(count):
            r0, c0 = corner(place)
            piece = pltpu.roll(gwin[place, part, pl.ds(pad - r0 + at, rows), :], c0, 1)
            low = low + jnp.where(lane >= c0, piece, 0.0)
            high = high + jnp.where(lane < c0, piece, 0.0)
        grad[part, pl.ds(at, rows), 0:width] = low
        grad[part, pl.ds(at, rows), width : 2 * width] = high

    def scatter_block(block, carry):
        for part in range(2):
            scatter_rows(part, pl.multiple_of(block * SCATTER_ROWS, SCATTER_ROWS))
        return carry

    def reduce_line(mode):
        got_p[mode, pl.ds(me_r, 1)] = pgrad[mode, pl.ds(me_r, 1)]
        finish([plane_copy(mode, step) for step in range(n_row - 1)])
        here = added(got_p.at[mode], n_row)
        total_p[mode] = here
        got_l[mode, pl.ds(me_c, 1)] = here[None]
        return to_line(total_p.at[mode], got_l.at[mode, me_c], rl_send.at[mode], rl_recv.at[mode])

    def spread(mode):
        full = added(got_l.at[mode], n_col)
        mine_at = pl.multiple_of(me_r * crow, crow)
        for k in range(2):
            at = pl.multiple_of((2 * mode + k) * width + mine_at, crow)
            old = probe_ref[pl.ds(at, crow), :]
            done = old - probe_rate * full[k * crow : (k + 1) * crow] / positions
            fresh[mode, k] = done
            new_probe_ref[2 * mode + k, pl.ds(mine_at, crow), :] = done
        return to_plane(
            lambda to: fresh.at[mode],
            new_probe_ref.at[pl.ds(2 * mode, 2), pl.ds(mine_at, crow)],
            g_send.at[mode], g_recv.at[mode],
        )


    for block in range(blocks):
        if block > 0:
            forward(block, 0)
        aim(block, 0)
    lax.fori_loop(0, count // BACKWARD, backward, 0)
    lax.fori_loop(0, n_row // PAIR, chunk_0, 0)
    lax.fori_loop(0, n_row // PAIR, chunk_1, 0)
    lax.fori_loop(0, count // 2, gather_modes, 0)
    lax.fori_loop(0, ext_rows // SCATTER_ROWS, scatter_block, 0)
    for i, (dr, dc) in enumerate(SIDES):
        start, rows = {-1: (0, half), 0: (half, tile), 1: (half + tile, half)}[dr]
        lc = 0 if dc == -1 else half + tile_c
        band = grad[:, start : start + rows, :][:, :, lc : lc + half]
        sides[i, 0:rows, :] = jnp.concatenate([band[0], band[1]], axis=-1)
    for i, (dr, dc) in enumerate(VERTS):
        start = 0 if dr == -1 else half + tile
        verts[i] = lanes_to(grad[:, start : start + half, :][:, :, half : half + tile_c], width)
    close, back = halo_back(
        n_row, n_col, sides, verts, near, back_sides, back_verts, b_send, b_recv, half
    )
    for copy in close:
        copy.start()
    lines = [reduce_line(mode) for mode in range(MODES)]
    finish(close)
    lo = pl.multiple_of((2 - 2 * lax.rem(me_r, 2)) // 2 * gap, gap)
    for k, dc in enumerate((-1, 1)):
        sides[SIDES.index((0, dc)), pl.ds(lo, half), :] += near[k]
    for copy in back:
        copy.start()
    squares = probe_ref[...]
    squares = squares * squares
    power = squares[0:width]
    for k in range(1, 4):
        power = power + squares[k * width : (k + 1) * width]
    power = jnp.max(jnp.max(power, axis=0, keepdims=True), axis=1, keepdims=True)
    rate = obj_rate / power
    kept = [grad[part, half : half + tile, :][:, half : half + tile_c] for part in range(2)]
    kept = [obj_ref[part] - rate * kept[part] for part in range(2)]
    gathers = []
    for mode in range(MODES):
        finish(lines[mode])
        gathers.append(spread(mode))
    finish(back)

    def grad_part(part):
        cut = slice(part * half, part * half + half)
        sums = None
        for dr, dc in SIDES + VERTS:
            rows = tile if dr == 0 else half
            if dc == 0:
                piece = back_verts[VERTS.index((dr, dc)), part][:, 0:tile_c]
            else:
                piece = back_sides[SIDES.index((dr, dc)), 0:rows, :][:, cut]
                fill = jnp.zeros((rows, gap_c), jnp.float32)
                piece = jnp.concatenate([fill, piece] if dc == -1 else [piece, fill], axis=1)
            if dr != 0:
                fill = jnp.zeros((gap, tile_c), jnp.float32)
                piece = jnp.concatenate([fill, piece] if dr == -1 else [piece, fill], axis=0)
            sums = piece if sums is None else sums + piece
        return sums

    for part in range(2):
        new_obj_ref[part] = kept[part] - rate * grad_part(part)
    for copies in gathers:
        finish(copies)


def settle_kernel(obj_ref, probe_ref, new_obj_ref, new_probe_ref, sems):
    copies = [
        pltpu.make_async_copy(obj_ref, new_obj_ref, sems.at[0]),
        pltpu.make_async_copy(probe_ref, new_probe_ref, sems.at[1]),
    ]
    for copy in copies:
        copy.start()
    for copy in copies:
        copy.wait()


def on_device(n_row, n_col, patterns, offsets, object_field, probe):
    pr, pc, width = patterns.shape[0], patterns.shape[1], patterns.shape[2]
    tile, tile_c = object_field.shape[1], object_field.shape[2]
    half = width // 2
    count = pr * pc
    lanes = 2 * width
    f32 = jnp.float32
    dma = pltpu.SemaphoreType.DMA
    side_shape, vert_shape = (len(SIDES), tile, width), (len(VERTS), 2, half, width)
    ext_rows = tile + 2 * half
    chunk = 2 * width // n_row
    tab, shift = tables(width)
    shapes = [
        side_shape, vert_shape, side_shape, vert_shape, side_shape, vert_shape, (2, half, width),
        (16, width), (n_row, 16, width), (16, width), (n_col, 16, width),
        (2, 2, ext_rows, width),
        (count, 2 * width, 2 * width),
        (count, 2, width, width),
        (count, width, width),
        (count, 2, width + 2 * tile, width),
        (2, ext_rows, lanes),
        (2, n_row, chunk, width),
        (2, count, width),
        (2, count, width),
        (count, width),
        (2, n_row, chunk, width),
        (2, chunk, width),
        (2, n_col, chunk, width),
        (2, 2, chunk // 2, width),
    ]
    sems = [
        (8,), (8,), (8,), (8,), (n_row - 1,), (n_row - 1,), (n_col - 1,), (n_col - 1,),
        (2, n_row - 1), (2, n_row - 1), (2, n_col - 1), (2, n_col - 1),
        (2, n_row - 1), (2, n_row - 1),
    ]
    new_object, new_probe = pl.pallas_call(
        functools.partial(whole_kernel, n_row, n_col, half, float(count * n_row * n_col)),
        out_shape=(
            pltpu.VMEM((2, tile, tile_c), f32),
            pltpu.VMEM((4, width, width), f32),
        ),
        in_specs=[ANY] * 6,
        out_specs=(VMEM, VMEM),
        scratch_shapes=[
            pltpu.VMEM((count, width, 2 * width), jnp.bfloat16),
            pltpu.VMEM((count, width), f32),
            pltpu.SMEM((pr, 2, pc), jnp.int32),
            pltpu.VMEM((count, width, width), f32),
            pltpu.VMEM((2, tile, tile_c), f32),
            pltpu.VMEM((4 * width, width), f32),
            pltpu.VMEM(tab.shape, jnp.bfloat16),
            pltpu.VMEM(shift.shape, f32),
            dma((6,)),
        ]
        + [pltpu.VMEM(shape, f32) for shape in shapes]
        + [dma(n) for n in sems],
        compiler_params=pltpu.CompilerParams(
            collective_id=0, has_side_effects=True, vmem_limit_bytes=60 * 1024 * 1024
        ),
        name="whole",
    )(
        jnp.transpose(offsets, (0, 2, 1)),
        patterns.reshape(count, width, width),
        object_field,
        probe.reshape(4 * width, width),
        jnp.asarray(tab),
        jnp.asarray(shift),
    )
    new_object, new_probe = pl.pallas_call(
        settle_kernel,
        out_shape=(
            jax.ShapeDtypeStruct((2, tile, tile_c), f32),
            jax.ShapeDtypeStruct((4, width, width), f32),
        ),
        in_specs=[VMEM] * 2,
        out_specs=(ANY, ANY),
        scratch_shapes=[dma((2,))],
        name="settle",
    )(
        pltpu.with_memory_space_constraint(new_object, pltpu.VMEM),
        pltpu.with_memory_space_constraint(new_probe, pltpu.VMEM),
    )
    return (new_object, new_probe.reshape(probe.shape))


def solution(mesh):
    placed = (P("srow", "scol", None, None), P("srow", "scol", None), P(None, "srow", "scol"), P())
    return jax.shard_map(
        functools.partial(on_device, mesh.shape["srow"], mesh.shape["scol"]),
        mesh=mesh,
        in_specs=placed,
        out_specs=(P(None, "srow", "scol"), P()),
        check_vma=False,
    )
```

```python
import functools
import math

import jax
import jax.numpy as jnp
import numpy as np
from jax import lax
from jax.experimental import pallas as pl
from jax.experimental.pallas import tpu as pltpu
from jax.sharding import PartitionSpec as P

MESH = pl.DeviceIdType.MESH
obj_rate = 0.2
probe_rate = 0.5
amp_floor = 0.1
GROUP = 4
FORWARD = 4
BACKWARD = 16
PAIR = 4
MODES = 2
tiny = 1e-30
SCATTER_ROWS = 40
DIRS = [(dr, dc) for dr in (-1, 0, 1) for dc in (-1, 0, 1) if (dr, dc) != (0, 0)]
SIDES = [d for d in DIRS if d[1] != 0]
VERTS = [d for d in DIRS if d[1] == 0]
VMEM = pl.BlockSpec(memory_space=pltpu.VMEM)
SMEM = pl.BlockSpec(memory_space=pltpu.SMEM)
ANY = pl.BlockSpec(memory_space=pl.ANY)


def split_np(table):
    high = table.astype(np.float32).astype(jnp.bfloat16)
    low = (table - high.astype(np.float64)).astype(np.float32).astype(jnp.bfloat16)
    return high, low


def tables(width):
    counter = np.arange(width)
    angles = 2.0 * np.pi / width * ((counter[:, None] * counter[None, :]) % width)
    cos, sin = np.cos(angles), np.sin(angles)
    plus = np.block([[cos, sin], [-sin, cos]])
    minus = np.block([[cos, -sin], [sin, cos]])
    scale = 1.0 / width
    parts = []
    for table in (minus * scale, plus, plus * scale, minus):
        parts.extend(split_np(table))
    shift = np.concatenate([cos, sin], axis=0) * scale
    return np.stack(parts), shift.astype(np.float32)


def split(values):
    high = values.astype(jnp.bfloat16)
    low = (values - high.astype(jnp.float32)).astype(jnp.bfloat16)
    return high, low


def mm(a, b):
    return jnp.dot(a, b, preferred_element_type=jnp.float32)


def signed(index, width):
    half = width // 2
    return jnp.where(index >= half, index - width, index).astype(jnp.float32)


def wrap(index, count):
    return lax.rem(index + count, count)


def greet(n_row, n_col):
    me_r, me_c = lax.axis_index("srow"), lax.axis_index("scol")
    barrier = pltpu.get_barrier_semaphore()

    def signal(row, col):
        pl.semaphore_signal(barrier, inc=1, device_id=(row, col), device_id_type=MESH)

    for k in range(1, n_col):
        signal(me_r, wrap(me_c + k, n_col))
    outer = wrap(me_r - 1 + 2 * lax.rem(me_r, 2), n_row)
    for dc in (-1, 1):
        signal(outer, wrap(me_c + dc, n_col))
    for k in range(1, n_row):
        signal(wrap(me_r + k, n_row), me_c)


def await_greetings(n_row, n_col):
    pl.semaphore_wait(pltpu.get_barrier_semaphore(), n_row - 1 + n_col - 1 + 2)


def copy_to(src, dst, send, recv, row, col):
    return pltpu.make_async_remote_copy(
        src_ref=src,
        dst_ref=dst,
        send_sem=send,
        recv_sem=recv,
        device_id=(row, col),
        device_id_type=MESH,
    )


def halo_out(n_row, n_col, sides, verts, got_sides, got_verts, send, recv, half):
    me_r, me_c = lax.axis_index("srow"), lax.axis_index("scol")
    toward = 1 - 2 * lax.rem(me_r, 2)
    strips, rest, passed = [], [], []
    for k, dc in enumerate((-1, 1)):
        col = wrap(me_c + dc, n_col)
        i = SIDES.index((0, dc))
        strips.append(copy_to(sides.at[i], got_sides.at[i], send.at[k], recv.at[k], me_r, col))
        i = (1 - toward) * 2 + (dc + 1) // 2
        src, dst = sides.at[i, pl.ds(0, half)], got_sides.at[i, pl.ds(0, half)]
        rest.append(copy_to(src, dst, send.at[2 + k], recv.at[2 + k], wrap(me_r - toward, n_row), col))
    for k, (dr, dc) in enumerate(VERTS):
        src, dst = verts.at[k], got_verts.at[k]
        rest.append(copy_to(src, dst, send.at[4 + k], recv.at[4 + k], wrap(me_r + dr, n_row), me_c))
    gap = sides.shape[1] - half
    lo = pl.multiple_of((1 + toward) // 2 * gap, gap)
    for k, dc in enumerate((-1, 1)):
        src = got_sides.at[SIDES.index((0, dc)), pl.ds(lo, half)]
        dst = got_sides.at[(1 + toward) * 2 + (dc + 1) // 2, pl.ds(0, half)]
        passed.append(copy_to(src, dst, send.at[6 + k], recv.at[6 + k], wrap(me_r + toward, n_row), me_c))
    return strips, rest, passed


def halo_back(n_row, n_col, sides, verts, near, back_sides, back_verts, send, recv, half):
    me_r, me_c = lax.axis_index("srow"), lax.axis_index("scol")
    toward = 1 - 2 * lax.rem(me_r, 2)
    close, far_off = [], []
    for k, dc in enumerate((-1, 1)):
        col = wrap(me_c + dc, n_col)
        src = sides.at[(1 + toward) * 2 + k, pl.ds(0, half)]
        close.append(copy_to(src, near.at[k], send.at[k], recv.at[k], wrap(me_r + toward, n_row), me_c))
        i = (1 - toward) * 2 + k
        src, dst = sides.at[i, pl.ds(0, half)], back_sides.at[i, pl.ds(0, half)]
        far_off.append(copy_to(src, dst, send.at[2 + k], recv.at[2 + k], wrap(me_r - toward, n_row), col))
        i = SIDES.index((0, dc))
        far_off.append(copy_to(sides.at[i], back_sides.at[i], send.at[4 + k], recv.at[4 + k], me_r, col))
    for k, (dr, dc) in enumerate(VERTS):
        src, dst = verts.at[k], back_verts.at[k]
        far_off.append(copy_to(src, dst, send.at[6 + k], recv.at[6 + k], wrap(me_r + dr, n_row), me_c))
    return close, far_off


def lanes_to(values, lanes):
    have = values.shape[-1]
    fill = jnp.zeros(values.shape[:-1] + (lanes - have,), values.dtype)
    return jnp.concatenate([values, fill], axis=-1)


def whole_kernel(
    n_row, n_col, half, positions,
    off_hbm, pat_hbm, obj_hbm, probe_hbm, tab_hbm, shift_hbm, new_obj_ref, new_probe_ref,
    pat_split, alts, off_ref, pat_ref, obj_ref, probe_ref, tab_ref, shift_ref, load_sems,
    sides, verts, got_sides, got_verts, back_sides, back_verts, near,
    sums, got_plane, total, got_line,
    ext, far, win, aims, gwin, grad, pgrad, desc_ref, kern, nyq,
    got_p, total_p, got_l, fresh,
    h_send, h_recv, b_send, b_recv, p_send, p_recv, z_send, z_recv,
    rp_send, rp_recv, rl_send, rl_recv, g_send, g_recv,
):
    greet(n_row, n_col)
    load_obj, load_pat, load_probe, load_tab, load_off, load_shift = [
        pltpu.make_async_copy(src, dst, load_sems.at[k])
        for k, (src, dst) in enumerate([
            (obj_hbm, obj_ref), (pat_hbm, pat_ref), (probe_hbm, probe_ref),
            (tab_hbm, tab_ref), (off_hbm, off_ref), (shift_hbm, shift_ref),
        ])
    ]
    for load in (load_pat, load_obj, load_probe, load_tab, load_off, load_shift):
        load.start()
    me_r, me_c = lax.axis_index("srow"), lax.axis_index("scol")
    pr, pc = off_ref.shape[0], off_ref.shape[2]
    count, width = pat_ref.shape[0], pat_ref.shape[1]
    tile, tile_c = obj_ref.shape[1], obj_ref.shape[2]
    gap, gap_c = tile - half, tile_c - half
    lanes = 2 * width
    ext_rows = ext.shape[2]
    load_obj.wait()
    for i, (dr, dc) in enumerate(SIDES):
        lo = gap if dr == 1 else 0
        rows = tile if dr == 0 else half
        lc = gap_c if dc == 1 else 0
        part = obj_ref[:, lo : lo + rows, :][:, :, lc : lc + half]
        sides[i, 0:rows, :] = jnp.concatenate([part[0], part[1]], axis=-1)
    for i, (dr, dc) in enumerate(VERTS):
        lo = gap if dr == 1 else 0
        verts[i] = lanes_to(obj_ref[:, lo : lo + half, :], width)
    def to_plane(src_of, dst, send, recv):
        copies = []
        for k in range(1, n_row):
            to = wrap(me_r + k, n_row)
            copies.append(copy_to(src_of(to), dst, send.at[k - 1], recv.at[k - 1], to, me_c))
        for copy in copies:
            copy.start()
        return copies

    def to_line(src, dst, send, recv):
        copies = []
        for k in range(1, n_col):
            to = wrap(me_c + k, n_col)
            copies.append(copy_to(src, dst, send.at[k - 1], recv.at[k - 1], me_r, to))
        for copy in copies:
            copy.start()
        return copies

    def finish(copies):
        for copy in copies:
            copy.wait()

    def added(ref, n):
        out = ref[0]
        for k in range(1, n):
            out = out + ref[k]
        return out

    odd = (
        lax.broadcasted_iota(jnp.int32, (width, width), 0)
        + lax.broadcasted_iota(jnp.int32, (width, width), 1)
    ) & 1
    signs = jnp.where(odd == 1, -1.0, 1.0).astype(jnp.float32)
    freq_k = signed(lax.broadcasted_iota(jnp.int32, (width, width), 0), width)
    freq_l = signed(lax.broadcasted_iota(jnp.int32, (1, width), 1), width)
    acc = [jnp.zeros((1, width), jnp.float32) for _ in range(9)]
    rows_all, cols_all = float(pr * n_row), float(pc * n_col)
    load_pat.wait()
    for r in range(pr):
        rho = ((me_r * pr + r).astype(jnp.float32) + 0.5) / rows_all - 0.5
        for c in range(pc):
            gam = ((me_c * pc + c).astype(jnp.float32) + 0.5) / cols_all - 0.5
            pattern = pat_ref[r * pc + c]
            col_sum = jnp.sum(pattern, axis=0, keepdims=True)
            row_mom = jnp.sum(pattern * freq_k, axis=0, keepdims=True)
            by_rho, by_gam = col_sum * rho, col_sum * gam
            new = [
                col_sum, by_rho, by_gam, by_rho * rho, by_rho * gam, by_gam * gam,
                row_mom, row_mom * rho, row_mom * gam,
            ]
            acc = [a + b for a, b in zip(acc, new)]
    pieces = acc + [acc[k] * freq_l for k in range(3)]
    stacked = jnp.concatenate(pieces + [jnp.zeros((4, width), jnp.float32)], axis=0)
    mine = jnp.broadcast_to(jnp.sum(stacked, axis=1, keepdims=True), stacked.shape)
    sums[...] = mine
    got_plane[pl.ds(me_r, 1)] = mine[None]
    await_greetings(n_row, n_col)
    strips, rest, passed = halo_out(
        n_row, n_col, sides, verts, got_sides, got_verts, h_send, h_recv, half
    )
    plane = to_plane(lambda to: sums, got_plane.at[me_r], p_send, p_recv)
    for copy in strips + rest:
        copy.start()
    for place in range(count):
        pattern = pat_ref[place]
        alts[place : place + 1, :] = jnp.sum(pattern * signs, axis=0, keepdims=True)
        high, low = split(pattern)
        pat_split[place] = jnp.concatenate([high, low], axis=1)
    pad = tile
    blank = jnp.zeros((count, 2, pad, width), jnp.float32)
    gwin[:, :, 0:pad, :] = blank
    back_sides[pl.ds(4 * lax.rem(me_r, 2), 2)] = jnp.zeros((2,) + back_sides.shape[1:], jnp.float32)
    gwin[:, :, pad + width :, :] = blank
    for load in (load_probe, load_tab, load_off, load_shift):
        load.wait()
    finish(plane)
    here = added(got_plane, n_row)
    total[...] = here
    got_line[pl.ds(me_c, 1)] = here[None]
    line = to_line(total, got_line.at[me_c], z_send, z_recv)
    for strip, onward in zip(strips, passed):
        strip.wait_recv()
        onward.start()
    for strip in strips:
        strip.wait_send()
    own = obj_ref[...]
    for dr, start, rows in ((0, half, tile), (1, 0, half), (-1, half + tile, half)):
        if dr == 1:
            finish(rest + passed)
        left_part = got_sides[SIDES.index((dr, 1)), 0:rows, :]
        right_part = got_sides[SIDES.index((dr, -1)), 0:rows, :]
        if dr == 0:
            middle = own
        else:
            middle = got_verts[VERTS.index((dr, 0))][:, :, 0:tile_c]
        for part in range(2):
            cut = slice(part * half, part * half + half)
            row = jnp.concatenate([left_part[:, cut], middle[part], right_part[:, cut]], axis=-1)
            row = lanes_to(row, lanes)
            ext[part, 0, start : start + rows, :] = row[:, :width]
            ext[part, 1, start : start + rows, :] = row[:, width:]

    def right(values, k):
        high, low = split(values)
        return mm(high, tab_ref[2 * k]) + mm(low, tab_ref[2 * k]) + mm(high, tab_ref[2 * k + 1])

    def left(values, k):
        high, low = split(values)
        return mm(tab_ref[2 * k], high) + mm(tab_ref[2 * k], low) + mm(tab_ref[2 * k + 1], high)

    def swap(values):
        top = jnp.concatenate([values[:width, :width], values[width:, :width]], axis=1)
        low = jnp.concatenate([values[:width, width:], values[width:, width:]], axis=1)
        return jnp.concatenate([top, low], axis=0)

    lane = lax.broadcasted_iota(jnp.int32, (1, width), 1)

    def corner(place):
        r, c = place // pc, place % pc
        return off_ref[r, 0, c], off_ref[r, 1, c]

    def window(part, r0, c0):
        shift = lax.rem(width - c0, width)
        first = pltpu.roll(ext[part, 0, pl.ds(r0, width), :], shift, 1)
        second = pltpu.roll(ext[part, 1, pl.ds(r0, width), :], shift, 1)
        return jnp.where(lane < width - c0, first, second)

    def forward(block, carry):
        places = [block * FORWARD + g for g in range(FORWARD)]
        p0r, p0i, p1r, p1i = (probe_ref[k * width : (k + 1) * width, :] for k in range(4))
        waves = []
        for place in places:
            r0, c0 = corner(place)
            wr, wi = window(0, r0, c0), window(1, r0, c0)
            win[place, 0] = wr
            win[place, 1] = wi
            top = jnp.concatenate([p0r * wr - p0i * wi, p0r * wi + p0i * wr], axis=1)
            low = jnp.concatenate([p1r * wr - p1i * wi, p1r * wi + p1i * wr], axis=1)
            waves.append(jnp.concatenate([top, low], axis=0))
        waves = [right(w, 0) for w in waves]
        for place, w in zip(places, waves):
            far[place] = left(swap(w), 1)
        return carry

    blocks = count // FORWARD
    forward(0, 0)
    finish(line)
    full = added(got_line, n_col)
    t = [full[k : k + 1, :] for k in range(12)]
    m = [[t[0], t[1], t[2]], [t[1], t[3], t[4]], [t[2], t[4], t[5]]]

    def cross(a, b):
        return [
            a[1] * b[2] - a[2] * b[1],
            a[2] * b[0] - a[0] * b[2],
            a[0] * b[1] - a[1] * b[0],
        ]

    crossed = [cross(m[1], m[2]), cross(m[2], m[0]), cross(m[0], m[1])]
    determ = m[0][0] * crossed[0][0] + m[0][1] * crossed[0][1] + m[0][2] * crossed[0][2]
    at = lax.broadcasted_iota(jnp.int32, (count, width), 0)
    at_r, at_c = at // pc, lax.rem(at, pc)
    rho = ((me_r * pr + at_r).astype(jnp.float32) + 0.5) / rows_all - 0.5
    gam = ((me_c * pc + at_c).astype(jnp.float32) + 0.5) / cols_all - 0.5
    pi = math.pi
    cos_tab, sin_tab = shift_ref[0:width, :], shift_ref[width : 2 * width, :]
    hi = lax.Precision.HIGHEST
    waves_of = []
    for axis in range(2):
        rhs = t[6 + 3 * axis : 9 + 3 * axis]
        coeff = [
            (crossed[0][i] * rhs[0] + crossed[1][i] * rhs[1] + crossed[2][i] * rhs[2]) / determ
            for i in range(3)
        ]
        desc = coeff[0] + rho * coeff[1] + gam * coeff[2]
        phase = desc * freq_l * (2.0 * pi / width)
        from_cos = jnp.dot(jnp.cos(phase), cos_tab, precision=hi, preferred_element_type=jnp.float32)
        from_sin = jnp.dot(jnp.sin(phase), sin_tab, precision=hi, preferred_element_type=jnp.float32)
        kern[axis] = from_cos + from_sin if axis == 0 else from_cos - from_sin
        waves_of.append(jnp.sin(desc * pi))
    alt = jnp.sum(alts[...], axis=1, keepdims=True)
    nyq[...] = waves_of[0] * waves_of[1] * alt * (1.0 / (width * width))
    def circulant(axis, place):
        row = kern[axis, pl.ds(place, 1), :]
        return pltpu.roll(
            jnp.broadcast_to(row, (width, width)), 0, 1, stride=1, stride_axis=0
        )

    def product(parts, values):
        high, low = split(values)
        top = jnp.concatenate([high, low], axis=1)
        bottom = jnp.concatenate([high, jnp.zeros_like(low)], axis=1)
        both = mm(parts, jnp.concatenate([top, bottom], axis=0))
        return both[:, :width] + both[:, width:]

    def target(place):
        first = product(pat_split[place], circulant(1, place))
        high, low = split(circulant(0, place))
        second = product(jnp.concatenate([high, low], axis=1), first)
        extra = nyq[pl.ds(place, 1), :]
        return jnp.maximum(second - extra * signs, 0.0)


    def aim(block, carry):
        places = [block * GROUP + g for g in range(GROUP)]
        goals = [target(place) for place in places]
        for place, goal in zip(places, goals):
            aims[place] = goal
        return carry

    def backward(block, carry):
        places = [block * BACKWARD + g for g in range(BACKWARD)]
        waves = []
        for place in places:
            f = far[place]
            power = f * f
            power = power[:width] + power[width:]
            power = jnp.maximum(power[:, :width] + power[:, width:], amp_floor * amp_floor)
            goal = aims[place]
            factor = 1.0 - goal * lax.rsqrt(jnp.maximum(goal, tiny) * power)
            factor = jnp.concatenate([factor, factor], axis=1)
            waves.append(jnp.concatenate([f[:width] * factor, f[width:] * factor], axis=0))
        waves = [left(w, 3) for w in waves]
        for place, w in zip(places, waves):
            far[place] = w
        return carry

    crow = width // n_row

    def owner_of(step):
        groups = n_row // PAIR
        at, flip = lax.rem(me_r, PAIR), PAIR - 1 - step % PAIR
        high = lax.rem(me_r // PAIR + groups - 1 - step // PAIR, groups)
        low, bit = 0, 1
        while bit < PAIR:
            low = low + lax.rem(at // bit + flip // bit, 2) * bit
            bit *= 2
        return high * PAIR + low

    def chunk_of(mode, pair):
        cut = slice(mode * width, (mode + 1) * width)
        steps = [PAIR * pair + k for k in range(PAIR)]
        owners = [owner_of(step) for step in steps]
        rows = []
        for owner in owners:
            at = pl.multiple_of(owner * crow, crow)
            for place in range(count):
                top = far[place, pl.ds(at, crow), cut]
                low = far[place, pl.ds(pl.multiple_of(width + at, crow), crow), cut]
                rows.append(jnp.concatenate([top, low], axis=1))
        waves = right(jnp.concatenate(rows, axis=0), 2)
        for n, owner in enumerate(owners):
            at = pl.multiple_of(owner * crow, crow)
            added_up = [None] * 2
            for place in range(count):
                wr, wi = win[place, 0, pl.ds(at, crow), :], win[place, 1, pl.ds(at, crow), :]
                lo = (n * count + place) * crow
                br, bi = waves[lo : lo + crow, :width], waves[lo : lo + crow, width:]
                parts = (wr * br + wi * bi, wr * bi - wi * br)
                for k in range(2):
                    added_up[k] = parts[k] if added_up[k] is None else added_up[k] + parts[k]
                far[place, pl.ds(at, crow), cut] = br
                far[place, pl.ds(pl.multiple_of(width + at, crow), crow), cut] = bi
            pgrad[mode, pl.ds(owner, 1)] = jnp.concatenate(added_up, axis=0)[None]
        for step in steps:

            @pl.when(step < n_row - 1)
            def _():
                plane_copy(mode, step).start()

    def gather_modes(block, carry):
        q = [probe_ref[k * width : (k + 1) * width, :] for k in range(4)]
        for place in [2 * block, 2 * block + 1]:
            gr, gi = None, None
            for mode in range(MODES):
                cut = slice(mode * width, (mode + 1) * width)
                br, bi = far[place, 0:width, cut], far[place, width : 2 * width, cut]
                qr, qi = q[2 * mode], q[2 * mode + 1]
                more_r, more_i = qr * br + qi * bi, qr * bi - qi * br
                gr = more_r if gr is None else gr + more_r
                gi = more_i if gi is None else gi + more_i
            gwin[place, 0, pad : pad + width, :] = gr
            gwin[place, 1, pad : pad + width, :] = gi
        return carry

    def chunk_0(step, carry):
        chunk_of(0, step)
        return carry

    def chunk_1(step, carry):
        chunk_of(1, step)
        return carry

    def plane_copy(mode, step):
        owner = owner_of(step)
        return copy_to(
            pgrad.at[mode, owner], got_p.at[mode, me_r],
            rp_send.at[mode, step], rp_recv.at[mode, step], owner, me_c,
        )

    def scatter_rows(part, at):
        rows = SCATTER_ROWS
        low = jnp.zeros((rows, width), jnp.float32)
        high = jnp.zeros((rows, width), jnp.float32)
        for place in range(count):
            r0, c0 = corner(place)
            piece = pltpu.roll(gwin[place, part, pl.ds(pad - r0 + at, rows), :], c0, 1)
            low = low + jnp.where(lane >= c0, piece, 0.0)
            high = high + jnp.where(lane < c0, piece, 0.0)
        grad[part, pl.ds(at, rows), 0:width] = low
        grad[part, pl.ds(at, rows), width : 2 * width] = high

    def scatter_block(block, carry):
        for part in range(2):
            scatter_rows(part, pl.multiple_of(block * SCATTER_ROWS, SCATTER_ROWS))
        return carry

    def reduce_line(mode):
        got_p[mode, pl.ds(me_r, 1)] = pgrad[mode, pl.ds(me_r, 1)]
        finish([plane_copy(mode, step) for step in range(n_row - 1)])
        here = added(got_p.at[mode], n_row)
        total_p[mode] = here
        got_l[mode, pl.ds(me_c, 1)] = here[None]
        return to_line(total_p.at[mode], got_l.at[mode, me_c], rl_send.at[mode], rl_recv.at[mode])

    def spread(mode):
        full = added(got_l.at[mode], n_col)
        mine_at = pl.multiple_of(me_r * crow, crow)
        for k in range(2):
            at = pl.multiple_of((2 * mode + k) * width + mine_at, crow)
            old = probe_ref[pl.ds(at, crow), :]
            done = old - probe_rate * full[k * crow : (k + 1) * crow] / positions
            fresh[mode, k] = done
            new_probe_ref[2 * mode + k, pl.ds(mine_at, crow), :] = done
        return to_plane(
            lambda to: fresh.at[mode],
            new_probe_ref.at[pl.ds(2 * mode, 2), pl.ds(mine_at, crow)],
            g_send.at[mode], g_recv.at[mode],
        )


    for block in range(blocks):
        if block > 0:
            forward(block, 0)
        aim(block, 0)
    lax.fori_loop(0, count // BACKWARD, backward, 0)
    lax.fori_loop(0, n_row // PAIR, chunk_0, 0)
    lax.fori_loop(0, n_row // PAIR, chunk_1, 0)
    lax.fori_loop(0, count // 2, gather_modes, 0)
    lax.fori_loop(0, ext_rows // SCATTER_ROWS, scatter_block, 0)
    for i, (dr, dc) in enumerate(SIDES):
        start, rows = {-1: (0, half), 0: (half, tile), 1: (half + tile, half)}[dr]
        lc = 0 if dc == -1 else half + tile_c
        band = grad[:, start : start + rows, :][:, :, lc : lc + half]
        sides[i, 0:rows, :] = jnp.concatenate([band[0], band[1]], axis=-1)
    for i, (dr, dc) in enumerate(VERTS):
        start = 0 if dr == -1 else half + tile
        verts[i] = lanes_to(grad[:, start : start + half, :][:, :, half : half + tile_c], width)
    close, back = halo_back(
        n_row, n_col, sides, verts, near, back_sides, back_verts, b_send, b_recv, half
    )
    for copy in close:
        copy.start()
    lines = [reduce_line(mode) for mode in range(MODES)]
    finish(close)
    lo = pl.multiple_of((2 - 2 * lax.rem(me_r, 2)) // 2 * gap, gap)
    for k, dc in enumerate((-1, 1)):
        sides[SIDES.index((0, dc)), pl.ds(lo, half), :] += near[k]
    for copy in back:
        copy.start()
    squares = probe_ref[...]
    squares = squares * squares
    power = squares[0:width]
    for k in range(1, 4):
        power = power + squares[k * width : (k + 1) * width]
    power = jnp.max(jnp.max(power, axis=0, keepdims=True), axis=1, keepdims=True)
    rate = obj_rate / power
    kept = [grad[part, half : half + tile, :][:, half : half + tile_c] for part in range(2)]
    kept = [obj_ref[part] - rate * kept[part] for part in range(2)]
    gathers = []
    for mode in range(MODES):
        finish(lines[mode])
        gathers.append(spread(mode))
    finish(back)

    def grad_part(part):
        cut = slice(part * half, part * half + half)
        sums = None
        for dr, dc in SIDES + VERTS:
            rows = tile if dr == 0 else half
            if dc == 0:
                piece = back_verts[VERTS.index((dr, dc)), part][:, 0:tile_c]
            else:
                piece = back_sides[SIDES.index((dr, dc)), 0:rows, :][:, cut]
                fill = jnp.zeros((rows, gap_c), jnp.float32)
                piece = jnp.concatenate([fill, piece] if dc == -1 else [piece, fill], axis=1)
            if dr != 0:
                fill = jnp.zeros((gap, tile_c), jnp.float32)
                piece = jnp.concatenate([fill, piece] if dr == -1 else [piece, fill], axis=0)
            sums = piece if sums is None else sums + piece
        return sums

    for part in range(2):
        new_obj_ref[part] = kept[part] - rate * grad_part(part)
    for copies in gathers:
        finish(copies)


def settle_kernel(obj_ref, probe_ref, new_obj_ref, new_probe_ref, sems):
    copies = [
        pltpu.make_async_copy(obj_ref, new_obj_ref, sems.at[0]),
        pltpu.make_async_copy(probe_ref, new_probe_ref, sems.at[1]),
    ]
    for copy in copies:
        copy.start()
    for copy in copies:
        copy.wait()


def on_device(n_row, n_col, patterns, offsets, object_field, probe):
    pr, pc, width = patterns.shape[0], patterns.shape[1], patterns.shape[2]
    tile, tile_c = object_field.shape[1], object_field.shape[2]
    half = width // 2
    count = pr * pc
    lanes = 2 * width
    f32 = jnp.float32
    dma = pltpu.SemaphoreType.DMA
    side_shape, vert_shape = (len(SIDES), tile, width), (len(VERTS), 2, half, width)
    ext_rows = tile + 2 * half
    chunk = 2 * width // n_row
    tab, shift = tables(width)
    shapes = [
        side_shape, vert_shape, side_shape, vert_shape, side_shape, vert_shape, (2, half, width),
        (16, width), (n_row, 16, width), (16, width), (n_col, 16, width),
        (2, 2, ext_rows, width),
        (count, 2 * width, 2 * width),
        (count, 2, width, width),
        (count, width, width),
        (count, 2, width + 2 * tile, width),
        (2, ext_rows, lanes),
        (2, n_row, chunk, width),
        (2, count, width),
        (2, count, width),
        (count, width),
        (2, n_row, chunk, width),
        (2, chunk, width),
        (2, n_col, chunk, width),
        (2, 2, chunk // 2, width),
    ]
    sems = [
        (8,), (8,), (8,), (8,), (n_row - 1,), (n_row - 1,), (n_col - 1,), (n_col - 1,),
        (2, n_row - 1), (2, n_row - 1), (2, n_col - 1), (2, n_col - 1),
        (2, n_row - 1), (2, n_row - 1),
    ]
    new_object, new_probe = pl.pallas_call(
        functools.partial(whole_kernel, n_row, n_col, half, float(count * n_row * n_col)),
        out_shape=(
            pltpu.VMEM((2, tile, tile_c), f32),
            pltpu.VMEM((4, width, width), f32),
        ),
        in_specs=[ANY] * 6,
        out_specs=(VMEM, VMEM),
        scratch_shapes=[
            pltpu.VMEM((count, width, 2 * width), jnp.bfloat16),
            pltpu.VMEM((count, width), f32),
            pltpu.SMEM((pr, 2, pc), jnp.int32),
            pltpu.VMEM((count, width, width), f32),
            pltpu.VMEM((2, tile, tile_c), f32),
            pltpu.VMEM((4 * width, width), f32),
            pltpu.VMEM(tab.shape, jnp.bfloat16),
            pltpu.VMEM(shift.shape, f32),
            dma((6,)),
        ]
        + [pltpu.VMEM(shape, f32) for shape in shapes]
        + [dma(n) for n in sems],
        compiler_params=pltpu.CompilerParams(
            collective_id=0, has_side_effects=True, vmem_limit_bytes=60 * 1024 * 1024
        ),
        name="whole",
    )(
        jnp.transpose(offsets, (0, 2, 1)),
        patterns.reshape(count, width, width),
        object_field,
        probe.reshape(4 * width, width),
        jnp.asarray(tab),
        jnp.asarray(shift),
    )
    new_object, new_probe = pl.pallas_call(
        settle_kernel,
        out_shape=(
            jax.ShapeDtypeStruct((2, tile, tile_c), f32),
            jax.ShapeDtypeStruct((4, width, width), f32),
        ),
        in_specs=[VMEM] * 2,
        out_specs=(ANY, ANY),
        scratch_shapes=[dma((2,))],
        name="settle",
    )(
        pltpu.with_memory_space_constraint(new_object, pltpu.VMEM),
        pltpu.with_memory_space_constraint(new_probe, pltpu.VMEM),
    )
    return (new_object, new_probe.reshape(probe.shape))


def solution(mesh):
    placed = (P("srow", "scol", None, None), P("srow", "scol", None), P(None, "srow", "scol"), P())
    return jax.shard_map(
        functools.partial(on_device, mesh.shape["srow"], mesh.shape["scol"]),
        mesh=mesh,
        in_specs=placed,
        out_specs=(P(None, "srow", "scol"), P()),
        check_vma=False,
    )
```

```python
import functools
import math

import jax
import jax.numpy as jnp
import numpy as np
from jax import lax
from jax.experimental import pallas as pl
from jax.experimental.pallas import tpu as pltpu
from jax.sharding import PartitionSpec as P

MESH = pl.DeviceIdType.MESH
obj_rate = 0.2
probe_rate = 0.5
amp_floor = 0.1
GROUP = 4
FORWARD = 4
BACKWARD = 16
PAIR = 4
MODES = 2
tiny = 1e-30
DIRS = [(dr, dc) for dr in (-1, 0, 1) for dc in (-1, 0, 1) if (dr, dc) != (0, 0)]
SIDES = [d for d in DIRS if d[1] != 0]
VERTS = [d for d in DIRS if d[1] == 0]
VMEM = pl.BlockSpec(memory_space=pltpu.VMEM)
SMEM = pl.BlockSpec(memory_space=pltpu.SMEM)
ANY = pl.BlockSpec(memory_space=pl.ANY)


def split_np(table):
    high = table.astype(np.float32).astype(jnp.bfloat16)
    low = (table - high.astype(np.float64)).astype(np.float32).astype(jnp.bfloat16)
    return high, low


def tables(width):
    counter = np.arange(width)
    angles = 2.0 * np.pi / width * ((counter[:, None] * counter[None, :]) % width)
    cos, sin = np.cos(angles), np.sin(angles)
    plus = np.block([[cos, sin], [-sin, cos]])
    minus = np.block([[cos, -sin], [sin, cos]])
    scale = 1.0 / width
    parts = []
    for table in (minus * scale, plus, plus * scale, minus):
        parts.extend(split_np(table))
    shift = np.concatenate([cos, sin], axis=0) * scale
    return np.stack(parts), shift.astype(np.float32)


def split(values):
    high = values.astype(jnp.bfloat16)
    low = (values - high.astype(jnp.float32)).astype(jnp.bfloat16)
    return high, low


def mm(a, b):
    return jnp.dot(a, b, preferred_element_type=jnp.float32)


def signed(index, width):
    half = width // 2
    return jnp.where(index >= half, index - width, index).astype(jnp.float32)


def wrap(index, count):
    return lax.rem(index + count, count)


def greet(n_row, n_col):
    me_r, me_c = lax.axis_index("srow"), lax.axis_index("scol")
    barrier = pltpu.get_barrier_semaphore()

    def signal(row, col):
        pl.semaphore_signal(barrier, inc=1, device_id=(row, col), device_id_type=MESH)

    for k in range(1, n_col):
        signal(me_r, wrap(me_c + k, n_col))
    outer = wrap(me_r - 1 + 2 * lax.rem(me_r, 2), n_row)
    for dc in (-1, 1):
        signal(outer, wrap(me_c + dc, n_col))
    for k in range(1, n_row):
        signal(wrap(me_r + k, n_row), me_c)


def await_greetings(n_row, n_col):
    pl.semaphore_wait(pltpu.get_barrier_semaphore(), n_row - 1 + n_col - 1 + 2)


def copy_to(src, dst, send, recv, row, col):
    return pltpu.make_async_remote_copy(
        src_ref=src,
        dst_ref=dst,
        send_sem=send,
        recv_sem=recv,
        device_id=(row, col),
        device_id_type=MESH,
    )


def halo_out(n_row, n_col, sides, verts, got_sides, got_verts, send, recv, half):
    me_r, me_c = lax.axis_index("srow"), lax.axis_index("scol")
    toward = 1 - 2 * lax.rem(me_r, 2)
    strips, rest, passed = [], [], []
    for k, dc in enumerate((-1, 1)):
        col = wrap(me_c + dc, n_col)
        i = SIDES.index((0, dc))
        strips.append(copy_to(sides.at[i], got_sides.at[i], send.at[k], recv.at[k], me_r, col))
        i = (1 - toward) * 2 + (dc + 1) // 2
        src, dst = sides.at[i, pl.ds(0, half)], got_sides.at[i, pl.ds(0, half)]
        rest.append(copy_to(src, dst, send.at[2 + k], recv.at[2 + k], wrap(me_r - toward, n_row), col))
    for k, (dr, dc) in enumerate(VERTS):
        src, dst = verts.at[k], got_verts.at[k]
        rest.append(copy_to(src, dst, send.at[4 + k], recv.at[4 + k], wrap(me_r + dr, n_row), me_c))
    gap = sides.shape[1] - half
    lo = pl.multiple_of((1 + toward) // 2 * gap, gap)
    for k, dc in enumerate((-1, 1)):
        src = got_sides.at[SIDES.index((0, dc)), pl.ds(lo, half)]
        dst = got_sides.at[(1 + toward) * 2 + (dc + 1) // 2, pl.ds(0, half)]
        passed.append(copy_to(src, dst, send.at[6 + k], recv.at[6 + k], wrap(me_r + toward, n_row), me_c))
    return strips, rest, passed


def halo_back(n_row, n_col, sides, verts, near, back_sides, back_verts, send, recv, half):
    me_r, me_c = lax.axis_index("srow"), lax.axis_index("scol")
    toward = 1 - 2 * lax.rem(me_r, 2)
    close, far_off = [], []
    for k, dc in enumerate((-1, 1)):
        col = wrap(me_c + dc, n_col)
        src = sides.at[(1 + toward) * 2 + k, pl.ds(0, half)]
        close.append(copy_to(src, near.at[k], send.at[k], recv.at[k], wrap(me_r + toward, n_row), me_c))
        i = (1 - toward) * 2 + k
        src, dst = sides.at[i, pl.ds(0, half)], back_sides.at[i, pl.ds(0, half)]
        far_off.append(copy_to(src, dst, send.at[2 + k], recv.at[2 + k], wrap(me_r - toward, n_row), col))
        i = SIDES.index((0, dc))
        far_off.append(copy_to(sides.at[i], back_sides.at[i], send.at[4 + k], recv.at[4 + k], me_r, col))
    for k, (dr, dc) in enumerate(VERTS):
        src, dst = verts.at[k], back_verts.at[k]
        far_off.append(copy_to(src, dst, send.at[6 + k], recv.at[6 + k], wrap(me_r + dr, n_row), me_c))
    return close, far_off


def lanes_to(values, lanes):
    have = values.shape[-1]
    fill = jnp.zeros(values.shape[:-1] + (lanes - have,), values.dtype)
    return jnp.concatenate([values, fill], axis=-1)


def whole_kernel(
    n_row, n_col, half, positions,
    off_hbm, pat_hbm, obj_hbm, probe_hbm, tab_hbm, shift_hbm, new_obj_ref, new_probe_ref,
    pat_split, alts, off_ref, pat_ref, obj_ref, probe_ref, tab_ref, shift_ref, load_sems,
    sides, verts, got_sides, got_verts, back_sides, back_verts, near,
    sums, got_plane, total, got_line,
    ext, far, win, aims, gwin, grad, pgrad, desc_ref, kern, nyq,
    got_p, total_p, got_l, fresh,
    h_send, h_recv, b_send, b_recv, p_send, p_recv, z_send, z_recv,
    rp_send, rp_recv, rl_send, rl_recv, g_send, g_recv,
):
    greet(n_row, n_col)
    load_obj, load_pat, load_probe, load_tab, load_off, load_shift = [
        pltpu.make_async_copy(src, dst, load_sems.at[k])
        for k, (src, dst) in enumerate([
            (obj_hbm, obj_ref), (pat_hbm, pat_ref), (probe_hbm, probe_ref),
            (tab_hbm, tab_ref), (off_hbm, off_ref), (shift_hbm, shift_ref),
        ])
    ]
    for load in (load_pat, load_obj, load_probe, load_tab, load_off, load_shift):
        load.start()
    me_r, me_c = lax.axis_index("srow"), lax.axis_index("scol")
    pr, pc = off_ref.shape[0], off_ref.shape[2]
    count, width = pat_ref.shape[0], pat_ref.shape[1]
    tile, tile_c = obj_ref.shape[1], obj_ref.shape[2]
    gap, gap_c = tile - half, tile_c - half
    lanes = 2 * width
    ext_rows = ext.shape[2]
    load_obj.wait()
    for i, (dr, dc) in enumerate(SIDES):
        lo = gap if dr == 1 else 0
        rows = tile if dr == 0 else half
        lc = gap_c if dc == 1 else 0
        part = obj_ref[:, lo : lo + rows, :][:, :, lc : lc + half]
        sides[i, 0:rows, :] = jnp.concatenate([part[0], part[1]], axis=-1)
    for i, (dr, dc) in enumerate(VERTS):
        lo = gap if dr == 1 else 0
        verts[i] = lanes_to(obj_ref[:, lo : lo + half, :], width)
    def to_plane(src_of, dst, send, recv):
        copies = []
        for k in range(1, n_row):
            to = wrap(me_r + k, n_row)
            copies.append(copy_to(src_of(to), dst, send.at[k - 1], recv.at[k - 1], to, me_c))
        for copy in copies:
            copy.start()
        return copies

    def to_line(src, dst, send, recv):
        copies = []
        for k in range(1, n_col):
            to = wrap(me_c + k, n_col)
            copies.append(copy_to(src, dst, send.at[k - 1], recv.at[k - 1], me_r, to))
        for copy in copies:
            copy.start()
        return copies

    def finish(copies):
        for copy in copies:
            copy.wait()

    def added(ref, n):
        out = ref[0]
        for k in range(1, n):
            out = out + ref[k]
        return out

    odd = (
        lax.broadcasted_iota(jnp.int32, (width, width), 0)
        + lax.broadcasted_iota(jnp.int32, (width, width), 1)
    ) & 1
    signs = jnp.where(odd == 1, -1.0, 1.0).astype(jnp.float32)
    freq_k = signed(lax.broadcasted_iota(jnp.int32, (width, width), 0), width)
    freq_l = signed(lax.broadcasted_iota(jnp.int32, (1, width), 1), width)
    acc = [jnp.zeros((1, width), jnp.float32) for _ in range(9)]
    rows_all, cols_all = float(pr * n_row), float(pc * n_col)
    load_pat.wait()
    for r in range(pr):
        rho = ((me_r * pr + r).astype(jnp.float32) + 0.5) / rows_all - 0.5
        for c in range(pc):
            gam = ((me_c * pc + c).astype(jnp.float32) + 0.5) / cols_all - 0.5
            pattern = pat_ref[r * pc + c]
            col_sum = jnp.sum(pattern, axis=0, keepdims=True)
            row_mom = jnp.sum(pattern * freq_k, axis=0, keepdims=True)
            by_rho, by_gam = col_sum * rho, col_sum * gam
            new = [
                col_sum, by_rho, by_gam, by_rho * rho, by_rho * gam, by_gam * gam,
                row_mom, row_mom * rho, row_mom * gam,
            ]
            acc = [a + b for a, b in zip(acc, new)]
    pieces = acc + [acc[k] * freq_l for k in range(3)]
    stacked = jnp.concatenate(pieces + [jnp.zeros((4, width), jnp.float32)], axis=0)
    mine = jnp.broadcast_to(jnp.sum(stacked, axis=1, keepdims=True), stacked.shape)
    sums[...] = mine
    got_plane[pl.ds(me_r, 1)] = mine[None]
    await_greetings(n_row, n_col)
    strips, rest, passed = halo_out(
        n_row, n_col, sides, verts, got_sides, got_verts, h_send, h_recv, half
    )
    plane = to_plane(lambda to: sums, got_plane.at[me_r], p_send, p_recv)
    for copy in strips + rest:
        copy.start()
    for place in range(count):
        pattern = pat_ref[place]
        alts[place : place + 1, :] = jnp.sum(pattern * signs, axis=0, keepdims=True)
        high, low = split(pattern)
        pat_split[place] = jnp.concatenate([high, low], axis=1)
    pad = tile
    blank = jnp.zeros((count, 2, pad, width), jnp.float32)
    gwin[:, :, 0:pad, :] = blank
    back_sides[pl.ds(4 * lax.rem(me_r, 2), 2)] = jnp.zeros((2,) + back_sides.shape[1:], jnp.float32)
    gwin[:, :, pad + width :, :] = blank
    for load in (load_probe, load_tab, load_off, load_shift):
        load.wait()
    finish(plane)
    here = added(got_plane, n_row)
    total[...] = here
    got_line[pl.ds(me_c, 1)] = here[None]
    line = to_line(total, got_line.at[me_c], z_send, z_recv)
    for strip, onward in zip(strips, passed):
        strip.wait_recv()
        onward.start()
    for strip in strips:
        strip.wait_send()
    own = obj_ref[...]
    for dr, start, rows in ((0, half, tile), (1, 0, half), (-1, half + tile, half)):
        if dr == 1:
            finish(rest + passed)
        left_part = got_sides[SIDES.index((dr, 1)), 0:rows, :]
        right_part = got_sides[SIDES.index((dr, -1)), 0:rows, :]
        if dr == 0:
            middle = own
        else:
            middle = got_verts[VERTS.index((dr, 0))][:, :, 0:tile_c]
        for part in range(2):
            cut = slice(part * half, part * half + half)
            row = jnp.concatenate([left_part[:, cut], middle[part], right_part[:, cut]], axis=-1)
            row = lanes_to(row, lanes)
            ext[part, 0, start : start + rows, :] = row[:, :width]
            ext[part, 1, start : start + rows, :] = row[:, width:]

    def right(values, k):
        high, low = split(values)
        return mm(high, tab_ref[2 * k]) + mm(low, tab_ref[2 * k]) + mm(high, tab_ref[2 * k + 1])

    def left(values, k):
        high, low = split(values)
        return mm(tab_ref[2 * k], high) + mm(tab_ref[2 * k], low) + mm(tab_ref[2 * k + 1], high)

    def swap(values):
        top = jnp.concatenate([values[:width, :width], values[width:, :width]], axis=1)
        low = jnp.concatenate([values[:width, width:], values[width:, width:]], axis=1)
        return jnp.concatenate([top, low], axis=0)

    lane = lax.broadcasted_iota(jnp.int32, (1, width), 1)

    def corner(place):
        r, c = place // pc, place % pc
        return off_ref[r, 0, c], off_ref[r, 1, c]

    def window(part, r0, c0):
        shift = lax.rem(width - c0, width)
        first = pltpu.roll(ext[part, 0, pl.ds(r0, width), :], shift, 1)
        second = pltpu.roll(ext[part, 1, pl.ds(r0, width), :], shift, 1)
        return jnp.where(lane < width - c0, first, second)

    def forward(block, carry):
        places = [block * FORWARD + g for g in range(FORWARD)]
        p0r, p0i, p1r, p1i = (probe_ref[k * width : (k + 1) * width, :] for k in range(4))
        waves = []
        for place in places:
            r0, c0 = corner(place)
            wr, wi = window(0, r0, c0), window(1, r0, c0)
            win[place, 0] = wr
            win[place, 1] = wi
            top = jnp.concatenate([p0r * wr - p0i * wi, p0r * wi + p0i * wr], axis=1)
            low = jnp.concatenate([p1r * wr - p1i * wi, p1r * wi + p1i * wr], axis=1)
            waves.append(jnp.concatenate([top, low], axis=0))
        waves = [right(w, 0) for w in waves]
        for place, w in zip(places, waves):
            far[place] = left(swap(w), 1)
        return carry

    blocks = count // FORWARD
    forward(0, 0)
    finish(line)
    full = added(got_line, n_col)
    t = [full[k : k + 1, :] for k in range(12)]
    m = [[t[0], t[1], t[2]], [t[1], t[3], t[4]], [t[2], t[4], t[5]]]

    def cross(a, b):
        return [
            a[1] * b[2] - a[2] * b[1],
            a[2] * b[0] - a[0] * b[2],
            a[0] * b[1] - a[1] * b[0],
        ]

    crossed = [cross(m[1], m[2]), cross(m[2], m[0]), cross(m[0], m[1])]
    determ = m[0][0] * crossed[0][0] + m[0][1] * crossed[0][1] + m[0][2] * crossed[0][2]
    at = lax.broadcasted_iota(jnp.int32, (count, width), 0)
    at_r, at_c = at // pc, lax.rem(at, pc)
    rho = ((me_r * pr + at_r).astype(jnp.float32) + 0.5) / rows_all - 0.5
    gam = ((me_c * pc + at_c).astype(jnp.float32) + 0.5) / cols_all - 0.5
    pi = math.pi
    cos_tab, sin_tab = shift_ref[0:width, :], shift_ref[width : 2 * width, :]
    hi = lax.Precision.HIGHEST
    waves_of = []
    for axis in range(2):
        rhs = t[6 + 3 * axis : 9 + 3 * axis]
        coeff = [
            (crossed[0][i] * rhs[0] + crossed[1][i] * rhs[1] + crossed[2][i] * rhs[2]) / determ
            for i in range(3)
        ]
        desc = coeff[0] + rho * coeff[1] + gam * coeff[2]
        phase = desc * freq_l * (2.0 * pi / width)
        from_cos = jnp.dot(jnp.cos(phase), cos_tab, precision=hi, preferred_element_type=jnp.float32)
        from_sin = jnp.dot(jnp.sin(phase), sin_tab, precision=hi, preferred_element_type=jnp.float32)
        kern[axis] = from_cos + from_sin if axis == 0 else from_cos - from_sin
        waves_of.append(jnp.sin(desc * pi))
    alt = jnp.sum(alts[...], axis=1, keepdims=True)
    nyq[...] = waves_of[0] * waves_of[1] * alt * (1.0 / (width * width))
    def circulant(axis, place):
        row = kern[axis, pl.ds(place, 1), :]
        return pltpu.roll(
            jnp.broadcast_to(row, (width, width)), 0, 1, stride=1, stride_axis=0
        )

    def product(parts, values):
        high, low = split(values)
        top = jnp.concatenate([high, low], axis=1)
        bottom = jnp.concatenate([high, jnp.zeros_like(low)], axis=1)
        both = mm(parts, jnp.concatenate([top, bottom], axis=0))
        return both[:, :width] + both[:, width:]

    def target(place):
        first = product(pat_split[place], circulant(1, place))
        high, low = split(circulant(0, place))
        second = product(jnp.concatenate([high, low], axis=1), first)
        extra = nyq[pl.ds(place, 1), :]
        return jnp.maximum(second - extra * signs, 0.0)


    def aim(block, carry):
        places = [block * GROUP + g for g in range(GROUP)]
        goals = [target(place) for place in places]
        for place, goal in zip(places, goals):
            aims[place] = goal
        return carry

    def backward(block, carry):
        places = [block * BACKWARD + g for g in range(BACKWARD)]
        waves = []
        for place in places:
            f = far[place]
            power = f * f
            power = power[:width] + power[width:]
            power = jnp.maximum(power[:, :width] + power[:, width:], amp_floor * amp_floor)
            goal = aims[place]
            factor = 1.0 - goal * lax.rsqrt(jnp.maximum(goal, tiny) * power)
            factor = jnp.concatenate([factor, factor], axis=1)
            waves.append(jnp.concatenate([f[:width] * factor, f[width:] * factor], axis=0))
        waves = [left(w, 3) for w in waves]
        for place, w in zip(places, waves):
            far[place] = w
        return carry

    crow = width // n_row

    def owner_of(step):
        groups = n_row // PAIR
        at, flip = lax.rem(me_r, PAIR), PAIR - 1 - step % PAIR
        high = lax.rem(me_r // PAIR + groups - 1 - step // PAIR, groups)
        low, bit = 0, 1
        while bit < PAIR:
            low = low + lax.rem(at // bit + flip // bit, 2) * bit
            bit *= 2
        return high * PAIR + low

    def chunk_of(mode, pair):
        cut = slice(mode * width, (mode + 1) * width)
        steps = [PAIR * pair + k for k in range(PAIR)]
        owners = [owner_of(step) for step in steps]
        rows = []
        for owner in owners:
            at = pl.multiple_of(owner * crow, crow)
            for place in range(count):
                top = far[place, pl.ds(at, crow), cut]
                low = far[place, pl.ds(pl.multiple_of(width + at, crow), crow), cut]
                rows.append(jnp.concatenate([top, low], axis=1))
        waves = right(jnp.concatenate(rows, axis=0), 2)
        for n, owner in enumerate(owners):
            at = pl.multiple_of(owner * crow, crow)
            added_up = [None] * 2
            for place in range(count):
                wr, wi = win[place, 0, pl.ds(at, crow), :], win[place, 1, pl.ds(at, crow), :]
                lo = (n * count + place) * crow
                br, bi = waves[lo : lo + crow, :width], waves[lo : lo + crow, width:]
                parts = (wr * br + wi * bi, wr * bi - wi * br)
                for k in range(2):
                    added_up[k] = parts[k] if added_up[k] is None else added_up[k] + parts[k]
                far[place, pl.ds(at, crow), cut] = br
                far[place, pl.ds(pl.multiple_of(width + at, crow), crow), cut] = bi
            pgrad[mode, pl.ds(owner, 1)] = jnp.concatenate(added_up, axis=0)[None]
        for step in steps:

            @pl.when(step < n_row - 1)
            def _():
                plane_copy(mode, step).start()

    def gather_modes(block, carry):
        q = [probe_ref[k * width : (k + 1) * width, :] for k in range(4)]
        for place in [2 * block, 2 * block + 1]:
            gr, gi = None, None
            for mode in range(MODES):
                cut = slice(mode * width, (mode + 1) * width)
                br, bi = far[place, 0:width, cut], far[place, width : 2 * width, cut]
                qr, qi = q[2 * mode], q[2 * mode + 1]
                more_r, more_i = qr * br + qi * bi, qr * bi - qi * br
                gr = more_r if gr is None else gr + more_r
                gi = more_i if gi is None else gi + more_i
            gwin[place, 0, pad : pad + width, :] = gr
            gwin[place, 1, pad : pad + width, :] = gi
        return carry

    def chunk_0(step, carry):
        chunk_of(0, step)
        return carry

    def chunk_1(step, carry):
        chunk_of(1, step)
        return carry

    def plane_copy(mode, step):
        owner = owner_of(step)
        return copy_to(
            pgrad.at[mode, owner], got_p.at[mode, me_r],
            rp_send.at[mode, step], rp_recv.at[mode, step], owner, me_c,
        )

    def scatter_rows(part, at):
        rows = ext_rows
        low = jnp.zeros((rows, width), jnp.float32)
        high = jnp.zeros((rows, width), jnp.float32)
        for place in range(count):
            r0, c0 = corner(place)
            piece = pltpu.roll(gwin[place, part, pl.ds(pad - r0 + at, rows), :], c0, 1)
            low = low + jnp.where(lane >= c0, piece, 0.0)
            high = high + jnp.where(lane < c0, piece, 0.0)
        grad[part, pl.ds(at, rows), 0:width] = low
        grad[part, pl.ds(at, rows), width : 2 * width] = high

    def scatter_block(block, carry):
        for part in range(2):
            scatter_rows(part, pl.multiple_of(block * ext_rows, ext_rows))
        return carry

    def reduce_line(mode):
        got_p[mode, pl.ds(me_r, 1)] = pgrad[mode, pl.ds(me_r, 1)]
        finish([plane_copy(mode, step) for step in range(n_row - 1)])
        here = added(got_p.at[mode], n_row)
        total_p[mode] = here
        got_l[mode, pl.ds(me_c, 1)] = here[None]
        return to_line(total_p.at[mode], got_l.at[mode, me_c], rl_send.at[mode], rl_recv.at[mode])

    def spread(mode):
        full = added(got_l.at[mode], n_col)
        mine_at = pl.multiple_of(me_r * crow, crow)
        for k in range(2):
            at = pl.multiple_of((2 * mode + k) * width + mine_at, crow)
            old = probe_ref[pl.ds(at, crow), :]
            done = old - probe_rate * full[k * crow : (k + 1) * crow] / positions
            fresh[mode, k] = done
            new_probe_ref[2 * mode + k, pl.ds(mine_at, crow), :] = done
        return to_plane(
            lambda to: fresh.at[mode],
            new_probe_ref.at[pl.ds(2 * mode, 2), pl.ds(mine_at, crow)],
            g_send.at[mode], g_recv.at[mode],
        )


    for block in range(blocks):
        if block > 0:
            forward(block, 0)
        aim(block, 0)
    lax.fori_loop(0, count // BACKWARD, backward, 0)
    lax.fori_loop(0, n_row // PAIR, chunk_0, 0)
    lax.fori_loop(0, n_row // PAIR, chunk_1, 0)
    lax.fori_loop(0, count // 2, gather_modes, 0)
    lax.fori_loop(0, 1, scatter_block, 0)
    for i, (dr, dc) in enumerate(SIDES):
        start, rows = {-1: (0, half), 0: (half, tile), 1: (half + tile, half)}[dr]
        lc = 0 if dc == -1 else half + tile_c
        band = grad[:, start : start + rows, :][:, :, lc : lc + half]
        sides[i, 0:rows, :] = jnp.concatenate([band[0], band[1]], axis=-1)
    for i, (dr, dc) in enumerate(VERTS):
        start = 0 if dr == -1 else half + tile
        verts[i] = lanes_to(grad[:, start : start + half, :][:, :, half : half + tile_c], width)
    close, back = halo_back(
        n_row, n_col, sides, verts, near, back_sides, back_verts, b_send, b_recv, half
    )
    for copy in close:
        copy.start()
    lines = [reduce_line(mode) for mode in range(MODES)]
    finish(close)
    lo = pl.multiple_of((2 - 2 * lax.rem(me_r, 2)) // 2 * gap, gap)
    for k, dc in enumerate((-1, 1)):
        sides[SIDES.index((0, dc)), pl.ds(lo, half), :] += near[k]
    for copy in back:
        copy.start()
    squares = probe_ref[...]
    squares = squares * squares
    power = squares[0:width]
    for k in range(1, 4):
        power = power + squares[k * width : (k + 1) * width]
    power = jnp.max(jnp.max(power, axis=0, keepdims=True), axis=1, keepdims=True)
    rate = obj_rate / power
    kept = [grad[part, half : half + tile, :][:, half : half + tile_c] for part in range(2)]
    kept = [obj_ref[part] - rate * kept[part] for part in range(2)]
    gathers = []
    for mode in range(MODES):
        finish(lines[mode])
        gathers.append(spread(mode))
    finish(back)

    def grad_part(part):
        cut = slice(part * half, part * half + half)
        sums = None
        for dr, dc in SIDES + VERTS:
            rows = tile if dr == 0 else half
            if dc == 0:
                piece = back_verts[VERTS.index((dr, dc)), part][:, 0:tile_c]
            else:
                piece = back_sides[SIDES.index((dr, dc)), 0:rows, :][:, cut]
                fill = jnp.zeros((rows, gap_c), jnp.float32)
                piece = jnp.concatenate([fill, piece] if dc == -1 else [piece, fill], axis=1)
            if dr != 0:
                fill = jnp.zeros((gap, tile_c), jnp.float32)
                piece = jnp.concatenate([fill, piece] if dr == -1 else [piece, fill], axis=0)
            sums = piece if sums is None else sums + piece
        return sums

    for part in range(2):
        new_obj_ref[part] = kept[part] - rate * grad_part(part)
    for copies in gathers:
        finish(copies)


def settle_kernel(obj_ref, probe_ref, new_obj_ref, new_probe_ref, sems):
    copies = [
        pltpu.make_async_copy(obj_ref, new_obj_ref, sems.at[0]),
        pltpu.make_async_copy(probe_ref, new_probe_ref, sems.at[1]),
    ]
    for copy in copies:
        copy.start()
    for copy in copies:
        copy.wait()


def on_device(n_row, n_col, patterns, offsets, object_field, probe):
    pr, pc, width = patterns.shape[0], patterns.shape[1], patterns.shape[2]
    tile, tile_c = object_field.shape[1], object_field.shape[2]
    half = width // 2
    count = pr * pc
    lanes = 2 * width
    f32 = jnp.float32
    dma = pltpu.SemaphoreType.DMA
    side_shape, vert_shape = (len(SIDES), tile, width), (len(VERTS), 2, half, width)
    ext_rows = tile + 2 * half
    chunk = 2 * width // n_row
    tab, shift = tables(width)
    shapes = [
        side_shape, vert_shape, side_shape, vert_shape, side_shape, vert_shape, (2, half, width),
        (16, width), (n_row, 16, width), (16, width), (n_col, 16, width),
        (2, 2, ext_rows, width),
        (count, 2 * width, 2 * width),
        (count, 2, width, width),
        (count, width, width),
        (count, 2, width + 2 * tile, width),
        (2, ext_rows, lanes),
        (2, n_row, chunk, width),
        (2, count, width),
        (2, count, width),
        (count, width),
        (2, n_row, chunk, width),
        (2, chunk, width),
        (2, n_col, chunk, width),
        (2, 2, chunk // 2, width),
    ]
    sems = [
        (8,), (8,), (8,), (8,), (n_row - 1,), (n_row - 1,), (n_col - 1,), (n_col - 1,),
        (2, n_row - 1), (2, n_row - 1), (2, n_col - 1), (2, n_col - 1),
        (2, n_row - 1), (2, n_row - 1),
    ]
    new_object, new_probe = pl.pallas_call(
        functools.partial(whole_kernel, n_row, n_col, half, float(count * n_row * n_col)),
        out_shape=(
            pltpu.VMEM((2, tile, tile_c), f32),
            pltpu.VMEM((4, width, width), f32),
        ),
        in_specs=[ANY] * 6,
        out_specs=(VMEM, VMEM),
        scratch_shapes=[
            pltpu.VMEM((count, width, 2 * width), jnp.bfloat16),
            pltpu.VMEM((count, width), f32),
            pltpu.SMEM((pr, 2, pc), jnp.int32),
            pltpu.VMEM((count, width, width), f32),
            pltpu.VMEM((2, tile, tile_c), f32),
            pltpu.VMEM((4 * width, width), f32),
            pltpu.VMEM(tab.shape, jnp.bfloat16),
            pltpu.VMEM(shift.shape, f32),
            dma((6,)),
        ]
        + [pltpu.VMEM(shape, f32) for shape in shapes]
        + [dma(n) for n in sems],
        compiler_params=pltpu.CompilerParams(
            collective_id=0, has_side_effects=True, vmem_limit_bytes=60 * 1024 * 1024
        ),
        name="whole",
    )(
        jnp.transpose(offsets, (0, 2, 1)),
        patterns.reshape(count, width, width),
        object_field,
        probe.reshape(4 * width, width),
        jnp.asarray(tab),
        jnp.asarray(shift),
    )
    new_object, new_probe = pl.pallas_call(
        settle_kernel,
        out_shape=(
            jax.ShapeDtypeStruct((2, tile, tile_c), f32),
            jax.ShapeDtypeStruct((4, width, width), f32),
        ),
        in_specs=[VMEM] * 2,
        out_specs=(ANY, ANY),
        scratch_shapes=[dma((2,))],
        name="settle",
    )(
        pltpu.with_memory_space_constraint(new_object, pltpu.VMEM),
        pltpu.with_memory_space_constraint(new_probe, pltpu.VMEM),
    )
    return (new_object, new_probe.reshape(probe.shape))


def solution(mesh):
    placed = (P("srow", "scol", None, None), P("srow", "scol", None), P(None, "srow", "scol"), P())
    return jax.shard_map(
        functools.partial(on_device, mesh.shape["srow"], mesh.shape["scol"]),
        mesh=mesh,
        in_specs=placed,
        out_specs=(P(None, "srow", "scol"), P()),
        check_vma=False,
    )
```
